512 devices in a mesh: seq: 32 (over z, core), head: 16 (over x, y).
Axes of the slice: x: 4, y: 4, z: 16, core: 2. Of those that a mesh axis runs over, the one named last changes fastest.
Arguments:
- queries: bfloat16 [16384, 2, 16, 128], P('seq', None, 'head'), may hold values from -2 to 2
- keys: bfloat16 [16384, 2, 128], P('seq'), may hold values from -2 to 2
- values: bfloat16 [16384, 2, 128], P('seq'), may hold values from -6 to 6
Outputs:
- attended: bfloat16 [16384, 2, 16, 128], P('seq', None, 'head')
The draws below stay inside these ranges and needn't reach their ends.
All inputs are finite; a program needn't handle non-finite values.
Results may differ from the reference program's by a relative error of at most 0.0058.
Values may be sent and summed in bfloat16 or wider, within the bound.
No kernel may reach another device: no remote copies, remote signals or barrier semaphores. Data moves between devices by JAX's collectives and lax.ppermute only.
A program may use at most 64 MiB of HBM per device.

```python
import math
import jax
import jax.numpy as jnp
import numpy as np
from jax import lax

DH = 128
GROUP = 16
KVH = 2
TOK_DEV = 512
FEAT = 8256
TOKENS = 16384


def level_of(stream_key, extent, split, least, high):
    loudness, own = 1.0, jax.random.fold_in(stream_key, 6)
    for axis_at, shards_of in split:
        steps = jnp.exp(jax.random.uniform(jax.random.fold_in(own, axis_at), (shards_of,), jnp.float32, least / len(split), high / len(split)))
        loudness = loudness * jnp.repeat(steps, extent[axis_at] // shards_of).reshape([-1 if axis == axis_at else 1 for axis in range(len(extent))])
    return loudness


def scatter_about(stream_key, extent, scale, reach, split=(), dtype=jnp.bfloat16):
    factor_of = level_of(stream_key, extent, split, -0.22, 0.18) if split else 1.0
    result = jax.random.normal(stream_key, extent, jnp.float32) * scale * factor_of
    return jnp.minimum(jnp.maximum(result, -reach), reach).astype(dtype)


def setup_inputs(seed: int = 0) -> dict:
    arg_keys = jax.random.split(jax.random.key(seed), 4)
    return {
        "queries": scatter_about(arg_keys[0], (TOKENS, KVH, GROUP, DH), 0.3, 2.0, ((0, 32), (2, 16))),
        "keys": scatter_about(arg_keys[1], (TOKENS, KVH, DH), 0.3, 2.0, ((0, 32),)),
        "values": scatter_about(arg_keys[2], (TOKENS, KVH, DH), 1.0, 6.0, ((0, 32),)),
    }


def feature_tables(head_width):
    row_index, col_index = np.triu_indices(head_width)
    pair_scale = np.where(row_index == col_index, 1.0, math.sqrt(2.0))
    return (jnp.asarray(row_index, jnp.int32), jnp.asarray(col_index, jnp.int32), jnp.asarray(pair_scale, jnp.float32))

def expand(source, row_index, col_index, pair_scale):
    return jnp.take(source, row_index, axis=-1) * jnp.take(source, col_index, axis=-1) * pair_scale

def wide_dot(left, right):
    return jnp.dot(left.astype(jnp.float32), right.astype(jnp.float32), preferred_element_type=jnp.float32, precision=lax.Precision.HIGHEST)

def reference(queries, keys, values):
    row_index, col_index, pair_scale = feature_tables(DH)
    span_count = queries.shape[0] // TOK_DEV
    q_spans = queries.reshape(span_count, TOK_DEV, KVH, GROUP, DH)
    k_spans = keys.reshape(span_count, TOK_DEV, KVH, DH)
    v_spans = values.reshape(span_count, TOK_DEV, KVH, DH)
    causal = jnp.tril(jnp.ones((TOK_DEV, TOK_DEV), jnp.float32))
    kv_ids = (jnp.arange(KVH * GROUP) // GROUP).astype(jnp.int32)

    def span_step(state, inputs):
        q_span, k_span, v_span = inputs
        k_phi = expand(k_span.astype(jnp.float32), row_index, col_index, pair_scale).astype(jnp.bfloat16)
        span_state = jnp.einsum('tkf,tkd->kfd', k_phi.astype(jnp.float32), v_span.astype(jnp.float32), precision=lax.Precision.HIGHEST)
        prefix_rounded = state.astype(jnp.bfloat16)
        per_head = q_span.reshape(TOK_DEV, KVH * GROUP, DH).transpose(1, 0, 2)

        def one_head(operands):
            q_head, kv_id = operands
            q_phi = expand(q_head.astype(jnp.float32), row_index, col_index, pair_scale).astype(jnp.bfloat16)
            cross = wide_dot(q_phi, prefix_rounded[kv_id])
            k_head = k_span[:, kv_id]
            v_head = v_span[:, kv_id]
            scores = wide_dot(q_head, k_head.T)
            weights = (scores * scores * causal).astype(jnp.bfloat16)
            own = wide_dot(weights, v_head)
            combined = cross + own
            factor = lax.rsqrt(lax.optimization_barrier(jnp.mean(combined * combined, axis=-1, keepdims=True)) + 1e-06)
            return (combined * factor).astype(jnp.bfloat16)
        outputs = lax.map(one_head, (per_head, kv_ids))
        outputs = outputs.transpose(1, 0, 2).reshape(TOK_DEV, KVH, GROUP, DH)
        return (state + span_state, outputs)
    initial = jnp.zeros((KVH, FEAT, DH), jnp.float32)
    final_state, attended = lax.scan(span_step, initial, (q_spans, k_spans, v_spans))
    return attended.reshape(queries.shape)
```

```python
import functools

import jax
import jax.numpy as jnp
from jax import lax
from jax.experimental import pallas as pl
from jax.experimental.pallas import tpu as pltpu
from jax.sharding import Mesh
from jax.sharding import PartitionSpec as P

DW = 128
CORES = ((0, 1), (1, 0))
SMEM = pltpu.MemorySpace.SMEM
VMEM = pltpu.MemorySpace.VMEM


def call(body, out_shape, n_in, scratch=(), flops=0, name=None):
    many = isinstance(out_shape, (list, tuple))
    vspec = pl.BlockSpec(memory_space=VMEM)
    return pl.pallas_call(
        body,
        out_shape=out_shape,
        in_specs=[pl.BlockSpec(memory_space=SMEM)] + [vspec] * n_in,
        out_specs=[vspec] * len(out_shape) if many else vspec,
        scratch_shapes=list(scratch),
        cost_estimate=pl.CostEstimate(flops=flops, transcendentals=0, bytes_accessed=1 << 20),
        name=name,
    )


def state_kernel(where_ref, mine_ref, theirs_ref, out_ref):
    slab = where_ref[1]
    keys = jnp.concatenate([mine_ref[0], theirs_ref[0]], axis=0).astype(jnp.float32).T
    values = jnp.concatenate([mine_ref[1], theirs_ref[1]], axis=0)
    homes, rows, _ = out_ref.shape
    for j in range(4):
        turn = slab * 4 + j
        factor = jnp.where(turn == 0, 1.0, 2.0)
        feats = (keys * pltpu.roll(keys, lax.rem(DW - turn, DW), axis=0) * factor).astype(jnp.bfloat16)
        state = jnp.dot(feats, values, preferred_element_type=jnp.float32).astype(jnp.bfloat16)
        for n in range(4):
            out_ref[4 * j + n, 0:32, :] = state[32 * n : 32 * n + 32]
    feats = (keys * pltpu.roll(keys, 64, axis=0)).astype(jnp.bfloat16)
    state = jnp.dot(feats, values, preferred_element_type=jnp.float32).astype(jnp.bfloat16)
    for n in range(homes):
        out_ref[n, 32:40, :] = state[8 * n : 8 * n + 8]


def prefix_kernel(where_ref, in_ref, out_ref):
    total = jnp.zeros(in_ref.shape[1:], jnp.float32)
    for n in range(in_ref.shape[0]):
        out_ref[n] = total.astype(jnp.bfloat16)
        total = total + in_ref[n].astype(jnp.float32)


def squared(q, k, v, causal):
    s = lax.dot_general(q, k, (((1,), (1,)), ((), ())), preferred_element_type=jnp.float32)
    s = s * s
    if causal:
        row = lax.broadcasted_iota(jnp.int32, s.shape, 0)
        col = lax.broadcasted_iota(jnp.int32, s.shape, 1)
        s = jnp.where(col <= row, s, 0.0)
    return jnp.dot(s.astype(jnp.bfloat16), v, preferred_element_type=jnp.float32)


def own_kernel(where_ref, q_ref, mine_ref, theirs_ref, out_ref, kv):
    core = where_ref[0]
    size = mine_ref.shape[1]
    kv[0] = mine_ref[...]
    kv[1] = theirs_ref[...]
    for h in range(2):
        out_ref[h] = squared(q_ref[h], kv[h, 0], kv[h, 1], True)
    late, early = 1 - core, core
    out_ref[late] += squared(q_ref[late], kv[early, 0], kv[early, 1], False)


def turned(q, turn):
    return (q * pltpu.roll(q, (DW - turn) % DW, axis=1) if turn % DW else q * q).astype(jnp.bfloat16)


TILE = 256


def cross_first(half, where_ref, q_ref, state_ref, own_ref, last_ref, out_ref):
    def tile(n, _):
        at = pl.ds(pl.multiple_of(n * TILE, TILE), TILE)
        q = q_ref[at, :].astype(jnp.float32)
        total = own_ref[at, :]
        total += jnp.dot(turned(q, 64), last_ref[...], preferred_element_type=jnp.float32)
        for p in range(16):
            feats = jnp.concatenate([turned(q, 4 * p + 2 * half), turned(q, 4 * p + 2 * half + 1)], axis=1)
            total += jnp.dot(feats, state_ref[p], preferred_element_type=jnp.float32)
        out_ref[at, :] = total
        return 0

    lax.fori_loop(0, q_ref.shape[0] // TILE, tile, 0)


def cross_second(half, where_ref, q_ref, state_ref, part_ref, out_ref):
    def tile(n, _):
        at = pl.ds(pl.multiple_of(n * TILE, TILE), TILE)
        q = q_ref[at, :].astype(jnp.float32)
        total = part_ref[at, :]
        for p in range(16):
            feats = jnp.concatenate([turned(q, 4 * p + 2 * half), turned(q, 4 * p + 2 * half + 1)], axis=1)
            total += jnp.dot(feats, state_ref[p], preferred_element_type=jnp.float32)
        mean = jnp.mean(total * total, axis=-1, keepdims=True)
        out_ref[at, :] = (total * lax.rsqrt(mean + 1e-06)).astype(jnp.bfloat16)
        return 0

    lax.fori_loop(0, q_ref.shape[0] // TILE, tile, 0)


def per_device(queries, keys, values):
    size = queries.shape[0]
    core = lax.axis_index("core")
    slab = lax.axis_index("x") * 4 + lax.axis_index("y")
    where = jnp.stack([core, slab]).astype(jnp.int32)
    first = core == 0
    bf16, f32 = jnp.bfloat16, jnp.float32
    shape = jax.ShapeDtypeStruct

    def split(a):
        return jnp.where(first, a[:, 0], a[:, 1]), jnp.where(first, a[:, 1], a[:, 0])

    k_mine, k_send = split(keys)
    v_mine, v_send = split(values)
    q_mine, q_send = split(queries[:, :, 0])
    mine = jnp.stack([k_mine, v_mine])
    theirs = lax.ppermute(jnp.stack([k_send, v_send]), "core", CORES)
    state = call(
        state_kernel, shape((16, 40, DW), bf16), 2, (), 10**9, "state"
    )(where, mine, theirs)
    blocks = lax.all_to_all(state, "z", 0, 0)
    q_theirs = lax.ppermute(q_send, "core", CORES)
    q_both = jnp.stack([q_mine, q_theirs])
    own = call(
        own_kernel, shape((2, size, DW), f32), 3, [pltpu.VMEM((2, 2, size, DW), bf16)], 10**9, "own"
    )(where, q_both, mine, theirs)
    prefix = call(prefix_kernel, shape((16, 40, DW), bf16), 1, (), 10**6, "prefix")(where, blocks)
    entering = lax.all_to_all(prefix, "z", 0, 0)
    last = entering[:, 32:].reshape(DW, DW)
    gathered = []
    for half in range(2):
        piece = entering[8 * half : 8 * half + 8, :32].reshape(256, DW)
        gathered.append(lax.all_to_all(jnp.broadcast_to(piece[None], (16, 256, DW)), ("x", "y"), 0, 0))
    q_flat = q_both.reshape(2 * size, DW)
    own = own.reshape(2 * size, DW)
    part = call(
        functools.partial(cross_first, 0), shape((2 * size, DW), f32), 4, (), 2 * 10**9, "cross_first"
    )(where, q_flat, gathered[0], own, last)
    done = call(
        functools.partial(cross_second, 1), shape((2 * size, DW), bf16), 3, (), 2 * 10**9, "cross_second"
    )(where, q_flat, gathered[1], part)
    here = done[:size]
    back = lax.ppermute(done[size:], "core", CORES)
    return jnp.where(first, jnp.stack([here, back], axis=1), jnp.stack([back, here], axis=1))[:, :, None]


def solution(mesh):
    grid = Mesh(mesh.devices.reshape(16, 2, 4, 4), ("z", "core", "x", "y"))
    seq, head = ("z", "core"), ("x", "y")
    return jax.shard_map(
        per_device,
        mesh=grid,
        in_specs=(P(seq, None, head, None), P(seq, None, None), P(seq, None, None)),
        out_specs=P(seq, None, head, None),
        check_vma=False,
    )
```

```python
import functools

import jax
import jax.numpy as jnp
from jax import lax
from jax.experimental import pallas as pl
from jax.experimental.pallas import tpu as pltpu
from jax.sharding import Mesh
from jax.sharding import PartitionSpec as P

DW = 128
TILE = 256
CORES = ((0, 1), (1, 0))
SMEM = pltpu.MemorySpace.SMEM
VMEM = pltpu.MemorySpace.VMEM
bf16, f32 = jnp.bfloat16, jnp.float32


def call(body, name, outs, where, ins, flops=0, scratch=()):
    vspec = pl.BlockSpec(memory_space=VMEM)
    return pl.pallas_call(
        body,
        out_shape=[pltpu.VMEM(s, d) for s, d in outs],
        in_specs=[pl.BlockSpec(memory_space=SMEM)] + [vspec] * len(ins),
        out_specs=[vspec] * len(outs),
        scratch_shapes=list(scratch),
        cost_estimate=pl.CostEstimate(flops=flops, transcendentals=0, bytes_accessed=1 << 20),
        compiler_params=pltpu.CompilerParams(vmem_limit_bytes=16 << 20),
        name=name,
    )(where, *[pltpu.with_memory_space_constraint(a, VMEM) for a in ins])


def state_kernel(where_ref, mine_ref, theirs_ref, out_ref):
    slab = where_ref[1]
    keys = jnp.concatenate([mine_ref[0], theirs_ref[0]], axis=0).astype(f32).T
    values = jnp.concatenate([mine_ref[1], theirs_ref[1]], axis=0)
    homes, rows, _ = out_ref.shape
    for j in range(4):
        turn = slab * 4 + j
        factor = jnp.where(turn == 0, 1.0, 2.0)
        feats = (keys * pltpu.roll(keys, lax.rem(DW - turn, DW), axis=0) * factor).astype(bf16)
        state = jnp.dot(feats, values, preferred_element_type=f32).astype(bf16)
        for n in range(4):
            out_ref[4 * j + n, 0:32, :] = state[32 * n : 32 * n + 32]
    feats = (keys * pltpu.roll(keys, 64, axis=0)).astype(bf16)
    state = jnp.dot(feats, values, preferred_element_type=f32).astype(bf16)
    for n in range(homes):
        out_ref[n, 32:40, :] = state[8 * n : 8 * n + 8]


def prefix_kernel(where_ref, in_ref, after_ref, out_ref):
    total = jnp.zeros(in_ref.shape[1:], f32)
    for n in range(in_ref.shape[0]):
        out_ref[n] = total.astype(bf16)
        total = total + in_ref[n].astype(f32)


def squared(q, k, v, causal):
    s = lax.dot_general(q, k, (((1,), (1,)), ((), ())), preferred_element_type=f32)
    s = s * s
    if causal:
        row = lax.broadcasted_iota(jnp.int32, s.shape, 0)
        col = lax.broadcasted_iota(jnp.int32, s.shape, 1)
        s = jnp.where(col <= row, s, 0.0)
    return jnp.dot(s.astype(bf16), v, preferred_element_type=f32)


def own_kernel(where_ref, q_ref, qt_ref, mine_ref, theirs_ref, out0_ref, out1_ref, after_ref, q, kv, out):
    core = where_ref[0]
    q[0], q[1] = q_ref[...], qt_ref[...]
    kv[0], kv[1] = mine_ref[...], theirs_ref[...]
    for h in range(2):
        out[h] = squared(q[h], kv[h, 0], kv[h, 1], True)
    late, early = 1 - core, core
    out[late] += squared(q[late], kv[early, 0], kv[early, 1], False)
    out0_ref[...], out1_ref[...] = out[0], out[1]
    after_ref[...] = jnp.zeros_like(after_ref)


def turned(q, turn):
    return q * pltpu.roll(q, (DW - turn) % DW, axis=1) if turn % DW else q * q


def spread_kernel(where_ref, in_ref, out_ref, last_ref):
    for n in range(16):
        piece = in_ref[n, 0:32, :]
        for p in range(16):
            out_ref[p, 32 * n : 32 * n + 32, :] = piece
        last_ref[8 * n : 8 * n + 8, :] = in_ref[n, 32:40, :]


def cross_kernel(where_ref, q_ref, state_ref, own_ref, last_ref, out_ref):
    def tile(n, _):
        at = pl.ds(pl.multiple_of(n * TILE, TILE), TILE)
        q = q_ref[at, :]
        total = own_ref[at, :]
        total += jnp.dot(turned(q, 64), last_ref[...], preferred_element_type=f32)
        for p in range(16):
            for j in range(0, 4, 2):
                feats = jnp.concatenate([turned(q, 4 * p + j), turned(q, 4 * p + j + 1)], axis=1)
                total += jnp.dot(feats, state_ref[p, DW * j : DW * (j + 2)], preferred_element_type=f32)
        mean = jnp.mean(total * total, axis=-1, keepdims=True)
        out_ref[at, :] = (total * lax.rsqrt(mean + 1e-06)).astype(bf16)
        return 0

    lax.fori_loop(0, q_ref.shape[0] // TILE, tile, 0)


def per_device(queries, keys, values):
    size = queries.shape[0]
    core = lax.axis_index("core")
    slab = lax.axis_index("x") * 4 + lax.axis_index("y")
    where = jnp.stack([core, slab]).astype(jnp.int32)
    first = core == 0

    def split(a):
        return jnp.where(first, a[:, 0], a[:, 1]), jnp.where(first, a[:, 1], a[:, 0])

    k_mine, k_send = split(keys)
    v_mine, v_send = split(values)
    q_mine, q_send = split(queries[:, :, 0])
    mine = jnp.stack([k_mine, v_mine])
    theirs = lax.ppermute(jnp.stack([k_send, v_send]), "core", CORES)
    (state,) = call(state_kernel, "state", [((16, 40, DW), bf16)], where, [mine, theirs], 10**9)
    blocks = lax.all_to_all(state, "z", 0, 0)
    q_theirs = lax.ppermute(q_send, "core", CORES)
    *own, after = call(
        own_kernel,
        "own",
        [((size, DW), f32), ((size, DW), f32), ((8, DW), f32)],
        where,
        [q_mine, q_theirs, mine, theirs],
        10**9,
        [pltpu.VMEM((2, size, DW), bf16), pltpu.VMEM((2, 2, size, DW), bf16), pltpu.VMEM((2, size, DW), f32)],
    )
    (prefix,) = call(prefix_kernel, "prefix", [((16, 40, DW), bf16)], where, [blocks, after], 10**6)
    entering = lax.all_to_all(prefix, "z", 0, 0)
    slabs, last = call(
        spread_kernel, "spread", [((16, 512, DW), bf16), ((DW, DW), bf16)], where, [entering], 10**6
    )
    gathered = lax.all_to_all(slabs, ("x", "y"), 0, 0)
    halves = []
    for n, q in ((1, q_theirs), (0, q_mine)):
        halves += call(cross_kernel, "cross", [((size, DW), bf16)], where, [q, gathered, own[n], last], 2 * 10**9)
        if n:
            back = lax.ppermute(halves[0], "core", CORES)
    here = halves[1]
    return jnp.where(first, jnp.stack([here, back], axis=1), jnp.stack([back, here], axis=1))[:, :, None]


def solution(mesh):
    grid = Mesh(mesh.devices.reshape(16, 2, 4, 4), ("z", "core", "x", "y"))
    seq, head = ("z", "core"), ("x", "y")
    return jax.shard_map(
        per_device,
        mesh=grid,
        in_specs=(P(seq, None, head, None), P(seq, None, None), P(seq, None, None)),
        out_specs=P(seq, None, head, None),
        check_vma=False,
    )
```

```python
import jax
import jax.numpy as jnp
from jax import lax
from jax.experimental import pallas as pl
from jax.experimental.pallas import tpu as pltpu
from jax.sharding import Mesh
from jax.sharding import PartitionSpec as P

DW = 128
CORES = ((0, 1), (1, 0))
SMEM = pltpu.MemorySpace.SMEM
VMEM = pltpu.MemorySpace.VMEM
bf16, f32 = jnp.bfloat16, jnp.float32


def call(body, name, outs, where, ins, flops=0, scratch=()):
    vspec = pl.BlockSpec(memory_space=VMEM)
    return pl.pallas_call(
        body,
        out_shape=[pltpu.VMEM(s, d) for s, d in outs],
        in_specs=[pl.BlockSpec(memory_space=SMEM)] + [vspec] * len(ins),
        out_specs=[vspec] * len(outs),
        scratch_shapes=list(scratch),
        cost_estimate=pl.CostEstimate(flops=flops, transcendentals=0, bytes_accessed=1 << 20),
        compiler_params=pltpu.CompilerParams(vmem_limit_bytes=16 << 20),
        name=name,
    )(where, *[pltpu.with_memory_space_constraint(a, VMEM) for a in ins])


def dot(a, b):
    return jnp.dot(a, b, preferred_element_type=f32)


def turned(x, turn, axis):
    return x * pltpu.roll(x, (DW - turn) % DW, axis=axis) if turn % DW else x * x


def state_kernel(where_ref, k_ref, v_ref, mine_ref, send_ref):
    core, slab = where_ref[0], where_ref[1]
    keys = k_ref[...]
    values = v_ref[...].astype(f32).T
    odd = lax.broadcasted_iota(jnp.int32, values.shape, 1) % 2
    both = jnp.concatenate(
        [jnp.where(odd == core, values, 0.0), jnp.where(odd == core, 0.0, values)], axis=0
    ).astype(bf16)
    for j in range(5):
        if j < 4:
            turn = slab * 4 + j
            factor = jnp.where(turn == 0, 1.0, 2.0).astype(bf16)
            feats = keys * pltpu.roll(keys, lax.rem(DW - turn, DW), axis=1) * factor
        else:
            feats = turned(keys, 64, 1)
        state = dot(both, feats)
        mine_ref[j] = state[:DW]
        send_ref[j] = state[DW:].astype(bf16)


def join_kernel(where_ref, mine_ref, got_ref, out_ref):
    for j in range(5):
        total = (mine_ref[j] + got_ref[j].astype(f32)).astype(bf16)
        if j < 4:
            for n in range(4):
                out_ref[4 * j + n, 0:32, :] = total[32 * n : 32 * n + 32]
        else:
            for n in range(16):
                out_ref[n, 32:40, :] = total[8 * n : 8 * n + 8]


def prefix_kernel(where_ref, in_ref, after_ref, out_ref):
    total = jnp.zeros(in_ref.shape[1:], f32)
    for n in range(in_ref.shape[0]):
        out_ref[n] = total.astype(bf16)
        total = total + in_ref[n].astype(f32)


def part_kernel(where_ref, q_ref, k_ref, v_ref, mine_ref, send_ref, rows):
    core = where_ref[0]
    for n, ref in enumerate((q_ref, k_ref, v_ref)):
        rows[...] = ref[...].astype(f32)
        even = rows[pl.ds(0, 512, stride=2), :].astype(bf16)
        odd = rows[pl.ds(1, 512, stride=2), :].astype(bf16)
        mine_ref[n] = jnp.where(core == 0, even, odd)
        send_ref[n] = jnp.where(core == 0, odd, even)


def squared(q, k, v, causal):
    s = lax.dot_general(k, q, (((1,), (1,)), ((), ())), preferred_element_type=f32)
    s = s * s
    if causal:
        source = lax.broadcasted_iota(jnp.int32, s.shape, 0)
        token = lax.broadcasted_iota(jnp.int32, s.shape, 1)
        s = jnp.where(source <= token, s, 0.0)
    return dot(v.astype(f32).T.astype(bf16), s.astype(bf16))


def own_kernel(where_ref, mine_ref, theirs_ref, out0_ref, out1_ref, after_ref, qkv, out):
    core = where_ref[0]
    qkv[0], qkv[1] = mine_ref[...], theirs_ref[...]
    for h in range(2):
        out[h] = squared(qkv[h, 0], qkv[h, 1], qkv[h, 2], True)
    late, early = 1 - core, core
    out[late] += squared(qkv[late, 0], qkv[early, 1], qkv[early, 2], False)
    out0_ref[...], out1_ref[...] = out[0], out[1]
    after_ref[...] = jnp.zeros_like(after_ref)


def spread_kernel(where_ref, in_ref, out_ref, last_ref):
    for n in range(16):
        piece = in_ref[n, 0:32, :]
        for p in range(16):
            out_ref[p, 32 * n : 32 * n + 32, :] = piece
        last_ref[8 * n : 8 * n + 8, :] = in_ref[n, 32:40, :]


def cross_kernel(where_ref, qkv_ref, state_ref, own_ref, last_ref, out_ref):
    q = qkv_ref[0].astype(f32).T.astype(bf16)
    total = own_ref[...] + dot(last_ref[...], turned(q, 64, 0))
    for p in range(16):
        feats = jnp.concatenate([turned(q, 4 * p + j, 0) for j in range(4)], axis=0)
        state = jnp.concatenate([state_ref[p, DW * j : DW * (j + 1)] for j in range(4)], axis=1)
        total += dot(state, feats)
    mean = jnp.mean(total * total, axis=0, keepdims=True)
    out_ref[...] = (total * lax.rsqrt(mean + 1e-06)).T.astype(bf16)


def per_device(queries, keys, values):
    size = queries.shape[0]
    core = lax.axis_index("core")
    slab = lax.axis_index("x") * 4 + lax.axis_index("y")
    where = jnp.stack([core, slab]).astype(jnp.int32)
    first = core == 0
    q, k, v = (a.reshape(2 * size, DW) for a in (queries, keys, values))
    mine, send = call(
        state_kernel, "state", [((5, DW, DW), f32), ((5, DW, DW), bf16)], where, [k, v], 10**9
    )
    got = lax.ppermute(send, "core", CORES)
    (state,) = call(join_kernel, "join", [((16, 40, DW), bf16)], where, [mine, got], 10**6)
    blocks = lax.all_to_all(state, "z", 0, 0)
    q, k, v, _ = lax.optimization_barrier((q, k, v, state))
    mine, send = call(
        part_kernel,
        "part",
        [((3, size, DW), bf16), ((3, size, DW), bf16)],
        where,
        [q, k, v],
        10**8,
        [pltpu.VMEM((2 * size, DW), f32)],
    )
    theirs = lax.ppermute(send, "core", CORES)
    *own, after = call(
        own_kernel,
        "own",
        [((DW, size), f32), ((DW, size), f32), ((8, DW), f32)],
        where,
        [mine, theirs],
        10**9,
        [pltpu.VMEM((2, 3, size, DW), bf16), pltpu.VMEM((2, DW, size), f32)],
    )
    (prefix,) = call(prefix_kernel, "prefix", [((16, 40, DW), bf16)], where, [blocks, after], 10**6)
    entering = lax.all_to_all(prefix, "z", 0, 0)
    slabs, last = call(
        spread_kernel, "spread", [((16, 512, DW), bf16), ((DW, DW), bf16)], where, [entering], 10**6
    )
    gathered = lax.all_to_all(slabs, ("x", "y"), 0, 0)
    halves = []
    for n, qkv in ((1, theirs), (0, mine)):
        halves += call(cross_kernel, "cross", [((size, DW), bf16)], where, [qkv, gathered, own[n], last], 2 * 10**9)
        if n:
            back = lax.ppermute(halves[0], "core", CORES)
    here = halves[1]
    return jnp.where(first, jnp.stack([here, back], axis=1), jnp.stack([back, here], axis=1))[:, :, None]


def solution(mesh):
    grid = Mesh(mesh.devices.reshape(16, 2, 4, 4), ("z", "core", "x", "y"))
    seq, head = ("z", "core"), ("x", "y")
    return jax.shard_map(
        per_device,
        mesh=grid,
        in_specs=(P(seq, None, head, None), P(seq, None, None), P(seq, None, None)),
        out_specs=P(seq, None, head, None),
        check_vma=False,
    )
```

```python
import jax
import jax.numpy as jnp
from jax import lax
from jax.experimental import pallas as pl
from jax.experimental.pallas import tpu as pltpu
from jax.sharding import Mesh
from jax.sharding import PartitionSpec as P

DW = 128
CORES = ((0, 1), (1, 0))
SMEM = pltpu.MemorySpace.SMEM
VMEM = pltpu.MemorySpace.VMEM
HBM = pltpu.MemorySpace.HBM
bf16, f32 = jnp.bfloat16, jnp.float32


def call(body, name, outs, where, ins, flops=0, scratch=(), raw=False, raw_out=False):
    ispec = pl.BlockSpec(memory_space=HBM if raw else VMEM)
    ospec = pl.BlockSpec(memory_space=HBM if raw_out else VMEM)
    return pl.pallas_call(
        body,
        out_shape=[(HBM if raw_out else VMEM)(s, d) for s, d in outs],
        in_specs=[pl.BlockSpec(memory_space=SMEM)] + [ispec] * len(ins),
        out_specs=[ospec] * len(outs),
        scratch_shapes=list(scratch),
        cost_estimate=pl.CostEstimate(flops=flops, transcendentals=0, bytes_accessed=1 << 20),
        compiler_params=pltpu.CompilerParams(vmem_limit_bytes=16 << 20),
        name=name,
    )(where, *[pltpu.with_memory_space_constraint(a, HBM if raw else VMEM) for a in ins])


def dot(a, b):
    return jnp.dot(a, b, preferred_element_type=f32)


def turned(x, turn, axis):
    return x * pltpu.roll(x, (DW - turn) % DW, axis=axis) if turn % DW else x * x


def state_kernel(where_ref, k_ref, v_ref, mine_ref, send_ref, k_buf, v_buf, sems):
    core, slab = where_ref[0], where_ref[1]
    copies = [pltpu.make_async_copy(r, b, sems.at[n]) for n, (r, b) in enumerate(((v_ref, v_buf), (k_ref, k_buf)))]
    for copy in copies:
        copy.start()
    copies[0].wait()
    values = v_buf[...].astype(f32).T
    odd = lax.broadcasted_iota(jnp.int32, values.shape, 1) % 2
    both = jnp.concatenate(
        [jnp.where(odd == core, values, 0.0), jnp.where(odd == core, 0.0, values)], axis=0
    ).astype(bf16)
    copies[1].wait()
    keys = k_buf[...]
    for j in range(5):
        if j < 4:
            turn = slab * 4 + j
            factor = jnp.where(turn == 0, 1.0, 2.0).astype(bf16)
            feats = keys * pltpu.roll(keys, lax.rem(DW - turn, DW), axis=1) * factor
        else:
            feats = turned(keys, 64, 1)
        state = dot(both, feats)
        mine_ref[j] = state[:DW]
        send_ref[j] = state[DW:].astype(bf16)


def join_kernel(where_ref, mine_ref, got_ref, out_ref):
    for j in range(5):
        total = (mine_ref[j] + got_ref[j].astype(f32)).astype(bf16)
        if j < 4:
            for n in range(4):
                out_ref[4 * j + n, 0:32, :] = total[32 * n : 32 * n + 32]
        else:
            for n in range(16):
                out_ref[n, 32:40, :] = total[8 * n : 8 * n + 8]


def prefix_kernel(where_ref, in_ref, after_ref, out_ref):
    total = jnp.zeros(in_ref.shape[1:], f32)
    for n in range(in_ref.shape[0]):
        out_ref[n] = total.astype(bf16)
        total = total + in_ref[n].astype(f32)


def part_kernel(where_ref, q_ref, k_ref, v_ref, mine_ref, send_ref, rows):
    core = where_ref[0]
    for n, ref in enumerate((q_ref, k_ref, v_ref)):
        rows[...] = ref[...].astype(f32)
        even = rows[pl.ds(0, 512, stride=2), :].astype(bf16)
        odd = rows[pl.ds(1, 512, stride=2), :].astype(bf16)
        mine_ref[n] = jnp.where(core == 0, even, odd)
        send_ref[n] = jnp.where(core == 0, odd, even)


def squared(q, k, v, causal):
    s = lax.dot_general(k, q, (((1,), (1,)), ((), ())), preferred_element_type=f32)
    s = s * s
    if causal:
        source = lax.broadcasted_iota(jnp.int32, s.shape, 0)
        token = lax.broadcasted_iota(jnp.int32, s.shape, 1)
        s = jnp.where(source <= token, s, 0.0)
    return dot(v.astype(f32).T.astype(bf16), s.astype(bf16))


def own_kernel(where_ref, mine_ref, theirs_ref, out0_ref, out1_ref, after_ref, qkv, out):
    core = where_ref[0]
    qkv[0], qkv[1] = mine_ref[...], theirs_ref[...]
    for h in range(2):
        out[h] = squared(qkv[h, 0], qkv[h, 1], qkv[h, 2], True)
    late, early = 1 - core, core
    out[late] += squared(qkv[late, 0], qkv[early, 1], qkv[early, 2], False)
    out0_ref[...], out1_ref[...] = out[0], out[1]
    after_ref[...] = jnp.zeros_like(after_ref)


def spread_kernel(where_ref, in_ref, out_ref, last_ref):
    for n in range(16):
        piece = in_ref[n, 0:32, :]
        for p in range(out_ref.shape[0]):
            out_ref[p, 32 * n : 32 * n + 32, :] = piece
        last_ref[8 * n : 8 * n + 8, :] = in_ref[n, 32:40, :]


def cross_kernel(where_ref, mine_ref, theirs_ref, pair_ref, state_ref, own0_ref, own1_ref, last_ref, out_ref):
    core, low = where_ref[0], where_ref[2]
    for block in range(2):
        for head in range(2):
            if head:
                q = pair_ref[block]
            else:
                q = (theirs_ref if block else mine_ref)[0]
            q = q.astype(f32).T.astype(bf16)
            ahead = jnp.where(low == 0, q, pltpu.roll(q, DW - 16, axis=0))
            if head:
                total = jnp.zeros((DW, q.shape[1]), f32)
            else:
                total = (own1_ref if block else own0_ref)[...] + dot(last_ref[...], turned(q, 64, 0))
            for p in range(8):
                turns = [32 * (p // 4) + 4 * (p % 4) + j for j in range(4)]
                feats = [q * (pltpu.roll(ahead, DW - t, axis=0) if t else ahead) for t in turns]
                state = [state_ref[p, DW * j : DW * (j + 1)] for j in range(4)]
                total += dot(jnp.concatenate(state, axis=1), jnp.concatenate(feats, axis=0))
            to_core = 1 - core if block else core
            to_low = 1 - low if head else low
            out_ref[2 * to_core + to_low] = total.astype(bf16)


def norm_kernel(where_ref, in_ref, out_ref, rows, buffer, sem):
    for kv in range(2):
        total = in_ref[2 * kv].astype(f32) + in_ref[2 * kv + 1].astype(f32)
        mean = jnp.mean(total * total, axis=0, keepdims=True)
        rows[pl.ds(kv, 512, stride=2), :] = (total * lax.rsqrt(mean + 1e-06)).T
    buffer[...] = rows[...].astype(bf16)
    copy = pltpu.make_async_copy(buffer, out_ref, sem)
    copy.start()
    copy.wait()


def per_device(queries, keys, values):
    size = queries.shape[0]
    core = lax.axis_index("core")
    low = lax.axis_index("xl")
    slab = lax.axis_index("xh") * 8 + low * 4 + lax.axis_index("y")
    where = jnp.stack([core, slab, low]).astype(jnp.int32)
    q, k, v = (a.reshape(2 * size, DW) for a in (queries, keys, values))
    buffer = pltpu.VMEM((2 * size, DW), bf16)
    mine, send = call(
        state_kernel,
        "state",
        [((5, DW, DW), f32), ((5, DW, DW), bf16)],
        where,
        [k, v],
        10**9,
        [buffer, buffer, pltpu.SemaphoreType.DMA((2,))],
        True,
    )
    got = lax.ppermute(send, "core", CORES)
    (state,) = call(join_kernel, "join", [((16, 40, DW), bf16)], where, [mine, got], 10**6)
    blocks = lax.all_to_all(state, "z", 0, 0)
    q, k, v, _ = lax.optimization_barrier((q, k, v, state))
    mine, send = call(
        part_kernel,
        "part",
        [((3, size, DW), bf16), ((3, size, DW), bf16)],
        where,
        [q, k, v],
        10**8,
        [pltpu.VMEM((2 * size, DW), f32)],
    )
    theirs = lax.ppermute(send, "core", CORES)
    pair = lax.ppermute(jnp.stack([mine[0], theirs[0]]), "xl", CORES)
    *own, after = call(
        own_kernel,
        "own",
        [((DW, size), f32), ((DW, size), f32), ((8, DW), f32)],
        where,
        [mine, theirs],
        10**9,
        [pltpu.VMEM((2, 3, size, DW), bf16), pltpu.VMEM((2, DW, size), f32)],
    )
    (prefix,) = call(prefix_kernel, "prefix", [((16, 40, DW), bf16)], where, [blocks, after], 10**6)
    entering = lax.all_to_all(prefix, "z", 0, 0)
    slabs, last = call(
        spread_kernel, "spread", [((8, 512, DW), bf16), ((DW, DW), bf16)], where, [entering], 10**6
    )
    gathered = lax.all_to_all(slabs, ("xh", "y"), 0, 0)
    (parts,) = call(
        cross_kernel,
        "cross",
        [((4, DW, size), bf16)],
        where,
        [mine, theirs, pair, gathered, *own, last],
        4 * 10**9,
    )
    parts = lax.all_to_all(parts, ("core", "xl"), 0, 0)
    (out,) = call(
        norm_kernel,
        "norm",
        [((2 * size, DW), bf16)],
        where,
        [parts],
        10**6,
        [pltpu.VMEM((2 * size, DW), f32), buffer, pltpu.SemaphoreType.DMA],
        raw_out=True,
    )
    return out.reshape(queries.shape)


def solution(mesh):
    grid = Mesh(mesh.devices.reshape(16, 2, 2, 2, 4), ("z", "core", "xh", "xl", "y"))
    seq, head = ("z", "core"), ("xh", "xl", "y")
    return jax.shard_map(
        per_device,
        mesh=grid,
        in_specs=(P(seq, None, head, None), P(seq, None, None), P(seq, None, None)),
        out_specs=P(seq, None, head, None),
        check_vma=False,
    )
```

```python
import jax
import jax.numpy as jnp
from jax import lax
from jax.experimental import pallas as pl
from jax.experimental.pallas import tpu as pltpu
from jax.sharding import Mesh
from jax.sharding import PartitionSpec as P

DW = 128
CORES = ((0, 1), (1, 0))
SMEM = pltpu.MemorySpace.SMEM
VMEM = pltpu.MemorySpace.VMEM
HBM = pltpu.MemorySpace.HBM
bf16, f32 = jnp.bfloat16, jnp.float32


def call(body, name, outs, where, ins, flops=0, scratch=(), raw=False, raw_out=False):
    ispec = pl.BlockSpec(memory_space=HBM if raw else VMEM)
    ospec = pl.BlockSpec(memory_space=HBM if raw_out else VMEM)
    return pl.pallas_call(
        body,
        out_shape=[(HBM if raw_out else VMEM)(s, d) for s, d in outs],
        in_specs=[pl.BlockSpec(memory_space=SMEM)] + [ispec] * len(ins),
        out_specs=[ospec] * len(outs),
        scratch_shapes=list(scratch),
        cost_estimate=pl.CostEstimate(flops=flops, transcendentals=0, bytes_accessed=1 << 20),
        compiler_params=pltpu.CompilerParams(vmem_limit_bytes=16 << 20),
        name=name,
    )(where, *[pltpu.with_memory_space_constraint(a, HBM if raw else VMEM) for a in ins])


def dot(a, b):
    return jnp.dot(a, b, preferred_element_type=f32)


def turned(x, turn, axis):
    return x * pltpu.roll(x, (DW - turn) % DW, axis=axis) if turn % DW else x * x


def state_kernel(where_ref, k_ref, v_ref, mine_ref, send_ref, k_buf, v_buf, sems):
    core, slab = where_ref[0], where_ref[1]
    copies = [pltpu.make_async_copy(r, b, sems.at[n]) for n, (r, b) in enumerate(((v_ref, v_buf), (k_ref, k_buf)))]
    for copy in copies:
        copy.start()
    copies[0].wait()
    values = v_buf[...].astype(f32).T
    odd = lax.broadcasted_iota(jnp.int32, values.shape, 1) % 2
    both = jnp.concatenate(
        [jnp.where(odd == core, values, 0.0), jnp.where(odd == core, 0.0, values)], axis=0
    ).astype(bf16)
    copies[1].wait()
    keys = k_buf[...]
    for j in range(5):
        if j < 4:
            turn = slab * 4 + j
            factor = jnp.where(turn == 0, 1.0, 2.0).astype(bf16)
            feats = keys * pltpu.roll(keys, lax.rem(DW - turn, DW), axis=1) * factor
        else:
            feats = turned(keys, 64, 1)
        state = dot(both, feats)
        mine_ref[j] = state[:DW]
        send_ref[j] = state[DW:].astype(bf16)


def join_kernel(where_ref, mine_ref, got_ref, out_ref):
    for j in range(5):
        total = (mine_ref[j] + got_ref[j].astype(f32)).astype(bf16)
        if j < 4:
            for n in range(4):
                out_ref[4 * j + n, 0:32, :] = total[32 * n : 32 * n + 32]
        else:
            for n in range(16):
                out_ref[n, 32:40, :] = total[8 * n : 8 * n + 8]


def prefix_kernel(where_ref, in_ref, after_ref, out_ref):
    total = jnp.zeros(in_ref.shape[1:], f32)
    for n in range(in_ref.shape[0]):
        out_ref[n] = total.astype(bf16)
        total = total + in_ref[n].astype(f32)


def part_kernel(where_ref, q_ref, k_ref, v_ref, mine_ref, send_ref, rows):
    core = where_ref[0]
    for n, ref in enumerate((q_ref, k_ref, v_ref)):
        rows[...] = ref[...].astype(f32)
        even = rows[pl.ds(0, 512, stride=2), :].astype(bf16)
        odd = rows[pl.ds(1, 512, stride=2), :].astype(bf16)
        mine_ref[n] = jnp.where(core == 0, even, odd)
        send_ref[n] = jnp.where(core == 0, odd, even)


def squared(q, k, v, causal):
    s = lax.dot_general(k, q, (((1,), (1,)), ((), ())), preferred_element_type=f32)
    s = s * s
    if causal:
        source = lax.broadcasted_iota(jnp.int32, s.shape, 0)
        token = lax.broadcasted_iota(jnp.int32, s.shape, 1)
        s = jnp.where(source <= token, s, 0.0)
    return dot(v.astype(f32).T.astype(bf16), s.astype(bf16))


def own_kernel(where_ref, mine_ref, theirs_ref, out0_ref, out1_ref, after_ref, qkv, out):
    core = where_ref[0]
    qkv[0], qkv[1] = mine_ref[...], theirs_ref[...]
    for h in range(2):
        out[h] = squared(qkv[h, 0], qkv[h, 1], qkv[h, 2], True)
    late, early = 1 - core, core
    out[late] += squared(qkv[late, 0], qkv[early, 1], qkv[early, 2], False)
    out0_ref[...], out1_ref[...] = out[0], out[1]
    after_ref[...] = jnp.zeros_like(after_ref)


def spread_kernel(where_ref, in_ref, pair_ref, out_ref, last_ref):
    for n in range(16):
        piece = in_ref[n, 0:32, :]
        for p in range(out_ref.shape[0]):
            out_ref[p, 32 * n : 32 * n + 32, :] = piece
        last_ref[8 * n : 8 * n + 8, :] = in_ref[n, 32:40, :]


def cross_kernel(where_ref, mine_ref, theirs_ref, pair_ref, state_ref, own0_ref, own1_ref, last_ref, out_ref):
    core, low = where_ref[0], where_ref[2]
    for block in range(2):
        for head in range(2):
            if head:
                q = pair_ref[block]
            else:
                q = (theirs_ref if block else mine_ref)[0]
            q = q.astype(f32).T.astype(bf16)
            ahead = jnp.where(low == 0, q, pltpu.roll(q, DW - 16, axis=0))
            if head:
                total = jnp.zeros((DW, q.shape[1]), f32)
            else:
                total = (own1_ref if block else own0_ref)[...] + dot(last_ref[...], turned(q, 64, 0))
            for p in range(8):
                turns = [32 * (p // 4) + 4 * (p % 4) + j for j in range(4)]
                feats = [q * (pltpu.roll(ahead, DW - t, axis=0) if t else ahead) for t in turns]
                state = [state_ref[p, DW * j : DW * (j + 1)] for j in range(4)]
                total += dot(jnp.concatenate(state, axis=1), jnp.concatenate(feats, axis=0))
            to_core = 1 - core if block else core
            to_low = 1 - low if head else low
            out_ref[2 * to_core + to_low] = total.astype(bf16)


def norm_kernel(where_ref, in_ref, out_ref, rows, buffer, sem):
    for kv in range(2):
        total = in_ref[2 * kv].astype(f32) + in_ref[2 * kv + 1].astype(f32)
        mean = jnp.mean(total * total, axis=0, keepdims=True)
        rows[pl.ds(kv, 512, stride=2), :] = (total * lax.rsqrt(mean + 1e-06)).T
    buffer[...] = rows[...].astype(bf16)
    copy = pltpu.make_async_copy(buffer, out_ref, sem)
    copy.start()
    copy.wait()


def per_device(queries, keys, values):
    size = queries.shape[0]
    core = lax.axis_index("core")
    low = lax.axis_index("xl")
    slab = lax.axis_index("xh") * 8 + low * 4 + lax.axis_index("y")
    where = jnp.stack([core, slab, low]).astype(jnp.int32)
    q, k, v = (a.reshape(2 * size, DW) for a in (queries, keys, values))
    buffer = pltpu.VMEM((2 * size, DW), bf16)
    mine, send = call(
        state_kernel,
        "state",
        [((5, DW, DW), f32), ((5, DW, DW), bf16)],
        where,
        [k, v],
        10**9,
        [buffer, buffer, pltpu.SemaphoreType.DMA((2,))],
        True,
    )
    got = lax.ppermute(send, "core", CORES)
    (state,) = call(join_kernel, "join", [((16, 40, DW), bf16)], where, [mine, got], 10**6)
    blocks = lax.all_to_all(state, "z", 0, 0)
    q, k, v, _ = lax.optimization_barrier((q, k, v, state))
    mine, send = call(
        part_kernel,
        "part",
        [((3, size, DW), bf16), ((3, size, DW), bf16)],
        where,
        [q, k, v],
        10**8,
        [pltpu.VMEM((2 * size, DW), f32)],
    )
    theirs = lax.ppermute(send, "core", CORES)
    pair = lax.ppermute(jnp.stack([mine[0], theirs[0]]), "xl", CORES)
    *own, after = call(
        own_kernel,
        "own",
        [((DW, size), f32), ((DW, size), f32), ((8, DW), f32)],
        where,
        [mine, theirs],
        10**9,
        [pltpu.VMEM((2, 3, size, DW), bf16), pltpu.VMEM((2, DW, size), f32)],
    )
    (prefix,) = call(prefix_kernel, "prefix", [((16, 40, DW), bf16)], where, [blocks, after], 10**6)
    entering = lax.all_to_all(prefix, "z", 0, 0)
    slabs, last = call(
        spread_kernel, "spread", [((8, 512, DW), bf16), ((DW, DW), bf16)], where, [entering, pair], 10**6
    )
    gathered = lax.all_to_all(slabs, ("xh", "y"), 0, 0)
    (parts,) = call(
        cross_kernel,
        "cross",
        [((4, DW, size), bf16)],
        where,
        [mine, theirs, pair, gathered, *own, last],
        4 * 10**9,
    )
    parts = lax.all_to_all(parts, ("core", "xl"), 0, 0)
    (out,) = call(
        norm_kernel,
        "norm",
        [((2 * size, DW), bf16)],
        where,
        [parts],
        10**6,
        [pltpu.VMEM((2 * size, DW), f32), buffer, pltpu.SemaphoreType.DMA],
        raw_out=True,
    )
    return out.reshape(queries.shape)


def solution(mesh):
    grid = Mesh(mesh.devices.reshape(16, 2, 2, 2, 4), ("z", "core", "xh", "xl", "y"))
    seq, head = ("z", "core"), ("xh", "xl", "y")
    return jax.shard_map(
        per_device,
        mesh=grid,
        in_specs=(P(seq, None, head, None), P(seq, None, None), P(seq, None, None)),
        out_specs=P(seq, None, head, None),
        check_vma=False,
    )
```

```python
import jax
import jax.numpy as jnp
from jax import lax
from jax.experimental import pallas as pl
from jax.experimental.pallas import tpu as pltpu
from jax.sharding import Mesh
from jax.sharding import PartitionSpec as P

DW = 128
CORES = ((0, 1), (1, 0))
SMEM = pltpu.MemorySpace.SMEM
VMEM = pltpu.MemorySpace.VMEM
HBM = pltpu.MemorySpace.HBM
bf16, f32 = jnp.bfloat16, jnp.float32


def call(body, name, outs, where, ins, flops=0, scratch=(), raw=False, raw_out=False):
    ispec = pl.BlockSpec(memory_space=HBM if raw else VMEM)
    ospec = pl.BlockSpec(memory_space=HBM if raw_out else VMEM)
    return pl.pallas_call(
        body,
        out_shape=[(HBM if raw_out else VMEM)(s, d) for s, d in outs],
        in_specs=[pl.BlockSpec(memory_space=SMEM)] + [ispec] * len(ins),
        out_specs=[ospec] * len(outs),
        scratch_shapes=list(scratch),
        cost_estimate=pl.CostEstimate(flops=flops, transcendentals=0, bytes_accessed=1 << 20),
        compiler_params=pltpu.CompilerParams(vmem_limit_bytes=16 << 20),
        name=name,
    )(where, *[pltpu.with_memory_space_constraint(a, HBM if raw else VMEM) for a in ins])


def dot(a, b):
    return jnp.dot(a, b, preferred_element_type=f32)


def turned(x, turn, axis):
    return x * pltpu.roll(x, (DW - turn) % DW, axis=axis) if turn % DW else x * x


def send_kernel(where_ref, k_ref, v_ref, send_ref, feats_ref, mine_ref, k_buf, v_buf, sems):
    core, slab = where_ref[0], where_ref[1]
    copies = [pltpu.make_async_copy(r, b, sems.at[n]) for n, (r, b) in enumerate(((v_ref, v_buf), (k_ref, k_buf)))]
    for copy in copies:
        copy.start()
    copies[0].wait()
    values = v_buf[...].astype(f32).T
    odd = lax.broadcasted_iota(jnp.int32, values.shape, 1) % 2
    mine_ref[...] = jnp.where(odd == core, values, 0.0).astype(bf16)
    others = jnp.where(odd == core, 0.0, values).astype(bf16)
    copies[1].wait()
    keys = k_buf[...]
    turns = []
    for j in range(4):
        turn = slab * 4 + j
        factor = jnp.where(turn == 0, 1.0, 2.0).astype(bf16)
        turns.append(keys * pltpu.roll(keys, lax.rem(DW - turn, DW), axis=1) * factor)
    turns.append(turned(keys, 64, 1))
    for j in range(0, 5, 2):
        feats = jnp.concatenate(turns[j : j + 2], axis=1)
        feats_ref[:, DW * j : DW * j + feats.shape[1]] = feats
        state = dot(others, feats).astype(bf16)
        for n in range(feats.shape[1] // DW):
            send_ref[j + n] = state[:, DW * n : DW * (n + 1)]


def mine_kernel(where_ref, feats_ref, values_ref, out_ref):
    for j in range(0, 5, 2):
        stop = min(5, j + 2)
        state = dot(values_ref[...], feats_ref[:, DW * j : DW * stop])
        for n in range(stop - j):
            out_ref[j + n] = state[:, DW * n : DW * (n + 1)]


def out_copies(buffer, out_ref, sems, n):
    copy = pltpu.make_async_copy(buffer.at[4 * n : 4 * n + 4], out_ref.at[4 * n : 4 * n + 4], sems.at[n])
    copy.start()
    return copy


def join_kernel(where_ref, mine_ref, got_ref, out_ref, buffer, sems):
    copies = []
    for j in (4, 0, 1, 2, 3):
        total = (mine_ref[j] + got_ref[j].astype(f32)).astype(bf16)
        if j < 4:
            for n in range(4):
                buffer[4 * j + n, 0:32, :] = total[32 * n : 32 * n + 32]
            copies.append(out_copies(buffer, out_ref, sems, j))
        else:
            for n in range(16):
                buffer[n, 32:40, :] = total[8 * n : 8 * n + 8]
    for copy in copies:
        copy.wait()


def prefix_kernel(where_ref, in_ref, after_ref, out_ref, buffer, sems):
    total = jnp.zeros(in_ref.shape[1:], f32)
    copies = []
    for n in range(in_ref.shape[0]):
        buffer[n] = total.astype(bf16)
        total = total + in_ref[n].astype(f32)
        if n % 4 == 3:
            copies.append(out_copies(buffer, out_ref, sems, n // 4))
    for copy in copies:
        copy.wait()


def part_kernel(where_ref, q_ref, k_ref, v_ref, mine_ref, send_ref, rows):
    core = where_ref[0]
    for n, ref in enumerate((q_ref, k_ref, v_ref)):
        rows[...] = ref[...].astype(f32)
        even = rows[pl.ds(0, 512, stride=2), :].astype(bf16)
        odd = rows[pl.ds(1, 512, stride=2), :].astype(bf16)
        mine_ref[n] = jnp.where(core == 0, even, odd)
        send_ref[n] = jnp.where(core == 0, odd, even)


def squared(q, k, v, causal):
    s = lax.dot_general(k, q, (((1,), (1,)), ((), ())), preferred_element_type=f32)
    s = s * s
    if causal:
        source = lax.broadcasted_iota(jnp.int32, s.shape, 0)
        token = lax.broadcasted_iota(jnp.int32, s.shape, 1)
        s = jnp.where(source <= token, s, 0.0)
    return dot(v.astype(f32).T.astype(bf16), s.astype(bf16))


def own_kernel(where_ref, mine_ref, theirs_ref, out0_ref, out1_ref, after_ref, qkv, out):
    core = where_ref[0]
    qkv[0], qkv[1] = mine_ref[...], theirs_ref[...]
    for h in range(2):
        out[h] = squared(qkv[h, 0], qkv[h, 1], qkv[h, 2], True)
    late, early = 1 - core, core
    out[late] += squared(qkv[late, 0], qkv[early, 1], qkv[early, 2], False)
    out0_ref[...], out1_ref[...] = out[0], out[1]
    after_ref[...] = jnp.zeros_like(after_ref)


def spread_kernel(where_ref, in_ref, pair_ref, out_ref, last_ref):
    for n in range(16):
        piece = in_ref[n, 0:32, :]
        for p in range(out_ref.shape[0]):
            out_ref[p, 32 * n : 32 * n + 32, :] = piece
        last_ref[8 * n : 8 * n + 8, :] = in_ref[n, 32:40, :]


def cross_kernel(where_ref, mine_ref, theirs_ref, pair_ref, state_ref, own0_ref, own1_ref, last_ref, out_ref):
    core, low = where_ref[0], where_ref[2]
    for block in range(2):
        for head in range(2):
            if head:
                q = pair_ref[block]
            else:
                q = (theirs_ref if block else mine_ref)[0]
            q = q.astype(f32).T.astype(bf16)
            ahead = jnp.where(low == 0, q, pltpu.roll(q, DW - 16, axis=0))
            if head:
                total = jnp.zeros((DW, q.shape[1]), f32)
            else:
                total = (own1_ref if block else own0_ref)[...] + dot(last_ref[...], turned(q, 64, 0))
            for p in range(8):
                turns = [32 * (p // 4) + 4 * (p % 4) + j for j in range(4)]
                feats = [q * (pltpu.roll(ahead, DW - t, axis=0) if t else ahead) for t in turns]
                state = [state_ref[p, DW * j : DW * (j + 1)] for j in range(4)]
                total += dot(jnp.concatenate(state, axis=1), jnp.concatenate(feats, axis=0))
            to_core = 1 - core if block else core
            to_low = 1 - low if head else low
            out_ref[2 * to_core + to_low] = total.astype(bf16)


def norm_kernel(where_ref, in_ref, out_ref, rows, buffer, sems):
    copies = []
    for n in range(2):
        at = slice(256 * n, 256 * n + 256)
        for kv in range(2):
            total = in_ref[2 * kv, :, at].astype(f32) + in_ref[2 * kv + 1, :, at].astype(f32)
            mean = jnp.mean(total * total, axis=0, keepdims=True)
            rows[pl.ds(512 * n + kv, 256, stride=2), :] = (total * lax.rsqrt(mean + 1e-06)).T
        at = slice(512 * n, 512 * n + 512)
        buffer[at, :] = rows[at, :].astype(bf16)
        copies.append(pltpu.make_async_copy(buffer.at[at], out_ref.at[at], sems.at[n]))
        copies[-1].start()
    for copy in copies:
        copy.wait()


def per_device(queries, keys, values):
    size = queries.shape[0]
    core = lax.axis_index("core")
    low = lax.axis_index("xl")
    slab = lax.axis_index("xh") * 8 + low * 4 + lax.axis_index("y")
    where = jnp.stack([core, slab, low]).astype(jnp.int32)
    q, k, v = (a.reshape(2 * size, DW) for a in (queries, keys, values))
    buffer = pltpu.VMEM((2 * size, DW), bf16)
    send, feats, kept = call(
        send_kernel,
        "send",
        [((5, DW, DW), bf16), ((2 * size, 5 * DW), bf16), ((DW, 2 * size), bf16)],
        where,
        [k, v],
        10**9,
        [buffer, buffer, pltpu.SemaphoreType.DMA((2,))],
        True,
    )
    got = lax.ppermute(send, "core", CORES)
    (mine,) = call(mine_kernel, "mine", [((5, DW, DW), f32)], where, [feats, kept], 10**9)
    chunks = [pltpu.VMEM((16, 40, DW), bf16), pltpu.SemaphoreType.DMA((4,))]
    (state,) = call(
        join_kernel, "join", [((16, 40, DW), bf16)], where, [mine, got], 10**6, chunks, raw_out=True
    )
    blocks = lax.all_to_all(state, "z", 0, 0)
    q, k, v, _ = lax.optimization_barrier((q, k, v, state))
    mine, send = call(
        part_kernel,
        "part",
        [((3, size, DW), bf16), ((3, size, DW), bf16)],
        where,
        [q, k, v],
        10**8,
        [pltpu.VMEM((2 * size, DW), f32)],
    )
    theirs = lax.ppermute(send, "core", CORES)
    pair = lax.ppermute(jnp.stack([mine[0], theirs[0]]), "xl", CORES)
    *own, after = call(
        own_kernel,
        "own",
        [((DW, size), f32), ((DW, size), f32), ((8, DW), f32)],
        where,
        [mine, theirs],
        10**9,
        [pltpu.VMEM((2, 3, size, DW), bf16), pltpu.VMEM((2, DW, size), f32)],
    )
    (prefix,) = call(
        prefix_kernel, "prefix", [((16, 40, DW), bf16)], where, [blocks, after], 10**6, chunks, raw_out=True
    )
    entering = lax.all_to_all(prefix, "z", 0, 0)
    slabs, last = call(
        spread_kernel, "spread", [((8, 512, DW), bf16), ((DW, DW), bf16)], where, [entering, pair], 10**6
    )
    gathered = lax.all_to_all(slabs, ("xh", "y"), 0, 0)
    (parts,) = call(
        cross_kernel,
        "cross",
        [((4, DW, size), bf16)],
        where,
        [mine, theirs, pair, gathered, *own, last],
        4 * 10**9,
    )
    parts = lax.all_to_all(parts, ("core", "xl"), 0, 0)
    (out,) = call(
        norm_kernel,
        "norm",
        [((2 * size, DW), bf16)],
        where,
        [parts],
        10**6,
        [pltpu.VMEM((2 * size, DW), f32), buffer, pltpu.SemaphoreType.DMA((2,))],
        raw_out=True,
    )
    return out.reshape(queries.shape)


def solution(mesh):
    grid = Mesh(mesh.devices.reshape(16, 2, 2, 2, 4), ("z", "core", "xh", "xl", "y"))
    seq, head = ("z", "core"), ("xh", "xl", "y")
    return jax.shard_map(
        per_device,
        mesh=grid,
        in_specs=(P(seq, None, head, None), P(seq, None, None), P(seq, None, None)),
        out_specs=P(seq, None, head, None),
        check_vma=False,
    )
```

```python
import jax
import jax.numpy as jnp
from jax import lax
from jax.experimental import pallas as pl
from jax.experimental.pallas import tpu as pltpu
from jax.sharding import Mesh
from jax.sharding import PartitionSpec as P


DW = 128
CORES = ((0, 1), (1, 0))
SMEM = pltpu.MemorySpace.SMEM
VMEM = pltpu.MemorySpace.VMEM
HBM = pltpu.MemorySpace.HBM
bf16, f32 = jnp.bfloat16, jnp.float32


def call(body, outs, where, ins, flops=0, scratch=(), raw=False, raw_out=False):
    ispec = pl.BlockSpec(memory_space=HBM if raw else VMEM)
    ospec = pl.BlockSpec(memory_space=HBM if raw_out else VMEM)
    return pl.pallas_call(
        body,
        out_shape=[(HBM if raw_out else VMEM)(s, d) for s, d in outs],
        in_specs=[pl.BlockSpec(memory_space=SMEM)] + [ispec] * len(ins),
        out_specs=[ospec] * len(outs),
        scratch_shapes=list(scratch),
        cost_estimate=pl.CostEstimate(flops=flops, transcendentals=0, bytes_accessed=1 << 20),
        compiler_params=pltpu.CompilerParams(vmem_limit_bytes=16 << 20),
    )(where, *[pltpu.with_memory_space_constraint(a, HBM if raw else VMEM) for a in ins])


def dot(a, b):
    return jnp.dot(a, b, preferred_element_type=f32)


def turned(x, turn, axis):
    return x * pltpu.roll(x, (DW - turn) % DW, axis=axis) if turn % DW else x * x


def send_kernel(where_ref, k_ref, v_ref, send_ref, feats_ref, mine_ref, k_buf, v_buf, sems):
    core, slab = where_ref[0], where_ref[1]
    copies = [pltpu.make_async_copy(r, b, sems.at[n]) for n, (r, b) in enumerate(((v_ref, v_buf), (k_ref, k_buf)))]
    for copy in copies:
        copy.start()
    copies[0].wait()
    values = v_buf[...].astype(f32).T
    odd = lax.broadcasted_iota(jnp.int32, values.shape, 1) % 2
    mine_ref[...] = jnp.where(odd == core, values, 0.0).astype(bf16)
    others = jnp.where(odd == core, 0.0, values).astype(bf16)
    copies[1].wait()
    keys = k_buf[...]
    turns = []
    for j in range(4):
        turn = slab * 4 + j
        factor = jnp.where(turn == 0, 1.0, 2.0).astype(bf16)
        turns.append(keys * pltpu.roll(keys, lax.rem(DW - turn, DW), axis=1) * factor)
    turns.append(turned(keys, 64, 1))
    for j in range(0, 5, 2):
        feats = jnp.concatenate(turns[j : j + 2], axis=1)
        feats_ref[:, DW * j : DW * j + feats.shape[1]] = feats
        state = dot(others, feats).astype(bf16)
        for n in range(feats.shape[1] // DW):
            send_ref[j + n] = state[:, DW * n : DW * (n + 1)]


def mine_kernel(where_ref, feats_ref, values_ref, out_ref):
    for j in range(0, 5, 2):
        stop = min(5, j + 2)
        state = dot(values_ref[...], feats_ref[:, DW * j : DW * stop])
        for n in range(stop - j):
            out_ref[j + n] = state[:, DW * n : DW * (n + 1)]


def out_copies(buffer, out_ref, sems, n):
    copy = pltpu.make_async_copy(buffer.at[2 * n : 2 * n + 2], out_ref.at[2 * n : 2 * n + 2], sems.at[n])
    copy.start()
    return copy


def join_kernel(where_ref, mine_ref, got_ref, out_ref):
    for j in range(5):
        total = (mine_ref[j] + got_ref[j].astype(f32)).astype(bf16)
        if j < 4:
            for n in range(2):
                out_ref[2 * j + n, 0:64, :] = total[64 * n : 64 * n + 64]
        else:
            for n in range(8):
                out_ref[n, 64:80, :] = total[16 * n : 16 * n + 16]


def total_kernel(where_ref, in_ref, out_ref):
    total = in_ref[0].astype(f32)
    for n in range(1, in_ref.shape[0]):
        total = total + in_ref[n].astype(f32)
    out_ref[...] = total


def prefix_kernel(where_ref, in_ref, before_ref, out_ref, buffer, sems):
    total = jnp.where(where_ref[3] == 0, 0.0, before_ref[...])
    copies = []
    for n in range(in_ref.shape[0]):
        buffer[n] = total.astype(bf16)
        total = total + in_ref[n].astype(f32)
        if n % 2:
            copies.append(out_copies(buffer, out_ref, sems, n // 2))
    for copy in copies:
        copy.wait()


def part_kernel(where_ref, q_ref, k_ref, v_ref, mine_ref, send_ref, rows):
    core = where_ref[0]
    for n, ref in enumerate((q_ref, k_ref, v_ref)):
        rows[...] = ref[...].astype(f32)
        even = rows[pl.ds(0, 512, stride=2), :].astype(bf16)
        odd = rows[pl.ds(1, 512, stride=2), :].astype(bf16)
        mine_ref[n] = jnp.where(core == 0, even, odd)
        send_ref[n] = jnp.where(core == 0, odd, even)


def squared(q, k, v, causal):
    s = lax.dot_general(k, q, (((1,), (1,)), ((), ())), preferred_element_type=f32)
    s = s * s
    if causal:
        source = lax.broadcasted_iota(jnp.int32, s.shape, 0)
        token = lax.broadcasted_iota(jnp.int32, s.shape, 1)
        s = jnp.where(source <= token, s, 0.0)
    return dot(v.astype(f32).T.astype(bf16), s.astype(bf16))


def own_kernel(where_ref, mine_ref, theirs_ref, out0_ref, out1_ref, qkv, out):
    core = where_ref[0]
    qkv[0], qkv[1] = mine_ref[...], theirs_ref[...]
    for h in range(2):
        out[h] = squared(qkv[h, 0], qkv[h, 1], qkv[h, 2], True)
    late, early = 1 - core, core
    out[late] += squared(qkv[late, 0], qkv[early, 1], qkv[early, 2], False)
    out0_ref[...], out1_ref[...] = out[0], out[1]


def spread_kernel(where_ref, in_ref, pair_ref, own_ref, out_ref, last_ref):
    for n in range(8):
        piece = in_ref[n, 0:64, :]
        for p in range(out_ref.shape[0]):
            out_ref[p, 64 * n : 64 * n + 64, :] = piece
        last_ref[16 * n : 16 * n + 16, :] = in_ref[n, 64:80, :]


def cross_kernel(where_ref, mine_ref, theirs_ref, pair_ref, state_ref, own0_ref, own1_ref, last_ref, out_ref):
    core, low = where_ref[0], where_ref[2]
    for block in range(2):
        for head in range(2):
            if head:
                q = pair_ref[block]
            else:
                q = (theirs_ref if block else mine_ref)[0]
            q = q.astype(f32).T.astype(bf16)
            ahead = jnp.where(low == 0, q, pltpu.roll(q, DW - 16, axis=0))
            if head:
                total = jnp.zeros((DW, q.shape[1]), f32)
            else:
                total = (own1_ref if block else own0_ref)[...] + dot(last_ref[...], turned(q, 64, 0))
            for p in range(8):
                turns = [32 * (p // 4) + 4 * (p % 4) + j for j in range(4)]
                feats = [q * (pltpu.roll(ahead, DW - t, axis=0) if t else ahead) for t in turns]
                state = [state_ref[p, DW * j : DW * (j + 1)] for j in range(4)]
                total += dot(jnp.concatenate(state, axis=1), jnp.concatenate(feats, axis=0))
            to_core = 1 - core if block else core
            to_low = 1 - low if head else low
            out_ref[2 * to_core + to_low] = total.astype(bf16)


def norm_kernel(where_ref, in_ref, out_ref, rows, buffer, sems):
    copies = []
    for n in range(2):
        at = slice(256 * n, 256 * n + 256)
        for kv in range(2):
            total = in_ref[2 * kv, :, at].astype(f32) + in_ref[2 * kv + 1, :, at].astype(f32)
            mean = jnp.mean(total * total, axis=0, keepdims=True)
            rows[pl.ds(512 * n + kv, 256, stride=2), :] = (total * lax.rsqrt(mean + 1e-06)).T
        at = slice(512 * n, 512 * n + 512)
        buffer[at, :] = rows[at, :].astype(bf16)
        copies.append(pltpu.make_async_copy(buffer.at[at], out_ref.at[at], sems.at[n]))
        copies[-1].start()
    for copy in copies:
        copy.wait()


def per_device(queries, keys, values):
    size = queries.shape[0]
    core = lax.axis_index("core")
    low = lax.axis_index("xl")
    slab = lax.axis_index("xh") * 8 + low * 4 + lax.axis_index("y")
    late = lax.axis_index("zh")
    where = jnp.stack([core, slab, low, late]).astype(jnp.int32)
    q, k, v = (a.reshape(2 * size, DW) for a in (queries, keys, values))
    buffer = pltpu.VMEM((2 * size, DW), bf16)
    send, feats, kept = call(
        send_kernel,
        [((5, DW, DW), bf16), ((2 * size, 5 * DW), bf16), ((DW, 2 * size), bf16)],
        where,
        [k, v],
        10**9,
        [buffer, buffer, pltpu.SemaphoreType.DMA((2,))],
        True,
    )
    got = lax.ppermute(send, "core", CORES)
    (mine,) = call(mine_kernel, [((5, DW, DW), f32)], where, [feats, kept], 10**9)
    chunks = ((8, 80, DW), bf16)
    (state,) = call(join_kernel, [chunks], where, [mine, got], 10**6)

    def exchange(state):
        return lax.all_to_all(state, "zl", 0, 0)

    def early(state):
        blocks = exchange(state)
        return blocks, call(total_kernel, [((80, DW), f32)], where, [blocks], 10**6)[0]

    def skip(state):
        return state, jnp.zeros((80, DW), f32)

    blocks, total = lax.cond(late == 0, early, skip, state)
    before = lax.ppermute(total, "zh", ((0, 1),))
    blocks = lax.cond(late == 0, lambda a: a, exchange, blocks)
    q, k, v, _ = lax.optimization_barrier((q, k, v, blocks))
    mine, send = call(
        part_kernel,
        [((3, size, DW), bf16), ((3, size, DW), bf16)],
        where,
        [q, k, v],
        10**8,
        [pltpu.VMEM((2 * size, DW), f32)],
    )
    theirs = lax.ppermute(send, "core", CORES)
    pair = lax.ppermute(jnp.stack([mine[0], theirs[0]]), "xl", CORES)
    own = call(
        own_kernel,
        [((DW, size), f32), ((DW, size), f32)],
        where,
        [mine, theirs],
        10**9,
        [pltpu.VMEM((2, 3, size, DW), bf16), pltpu.VMEM((2, DW, size), f32)],
    )
    (prefix,) = call(
        prefix_kernel,
        [chunks],
        where,
        [blocks, before],
        10**6,
        [pltpu.VMEM(*chunks), pltpu.SemaphoreType.DMA((4,))],
        raw_out=True,
    )
    entering = exchange(prefix)
    slabs, last = call(spread_kernel, [((8, 512, DW), bf16), ((DW, DW), bf16)], where, [entering, pair, own[0]], 10**6)
    gathered = lax.all_to_all(slabs, ("xh", "y"), 0, 0)
    (parts,) = call(cross_kernel, [((4, DW, size), bf16)], where, [mine, theirs, pair, gathered, *own, last], 4 * 10**9)
    parts = lax.all_to_all(parts, ("core", "xl"), 0, 0)
    (out,) = call(
        norm_kernel,
        [((2 * size, DW), bf16)],
        where,
        [parts],
        10**6,
        [pltpu.VMEM((2 * size, DW), f32), buffer, pltpu.SemaphoreType.DMA((2,))],
        raw_out=True,
    )
    return out.reshape(queries.shape)


def solution(mesh):
    grid = Mesh(mesh.devices.reshape(2, 8, 2, 2, 2, 4), ("zh", "zl", "core", "xh", "xl", "y"))
    seq, head = ("zh", "zl", "core"), ("xh", "xl", "y")
    return jax.shard_map(
        per_device,
        mesh=grid,
        in_specs=(P(seq, None, head, None), P(seq, None, None), P(seq, None, None)),
        out_specs=P(seq, None, head, None),
        check_vma=False,
    )
```

```python
import jax
import jax.numpy as jnp
from jax import lax
from jax.experimental import pallas as pl
from jax.experimental.pallas import tpu as pltpu
from jax.sharding import Mesh
from jax.sharding import PartitionSpec as P


DW = 128
CORES = ((0, 1), (1, 0))
SMEM = pltpu.MemorySpace.SMEM
VMEM = pltpu.MemorySpace.VMEM
HBM = pltpu.MemorySpace.HBM
bf16, f32 = jnp.bfloat16, jnp.float32


def call(body, outs, where, ins, flops=0, scratch=(), raw=False, raw_out=False):
    ispec = pl.BlockSpec(memory_space=HBM if raw else VMEM)
    ospec = pl.BlockSpec(memory_space=HBM if raw_out else VMEM)
    return pl.pallas_call(
        body,
        out_shape=[(HBM if raw_out else VMEM)(s, d) for s, d in outs],
        in_specs=[pl.BlockSpec(memory_space=SMEM)] + [ispec] * len(ins),
        out_specs=[ospec] * len(outs),
        scratch_shapes=list(scratch),
        cost_estimate=pl.CostEstimate(flops=flops, transcendentals=0, bytes_accessed=1 << 20),
        compiler_params=pltpu.CompilerParams(vmem_limit_bytes=16 << 20),
    )(where, *[pltpu.with_memory_space_constraint(a, HBM if raw else VMEM) for a in ins])


def dot(a, b):
    return jnp.dot(a, b, preferred_element_type=f32)


def turned(x, turn, axis):
    return x * pltpu.roll(x, (DW - turn) % DW, axis=axis) if turn % DW else x * x


def send_kernel(where_ref, k_ref, v_ref, send_ref, feats_ref, mine_ref, k_buf, v_buf, sems):
    core, slab = where_ref[0], where_ref[1]
    copies = [pltpu.make_async_copy(r, b, sems.at[n]) for n, (r, b) in enumerate(((v_ref, v_buf), (k_ref, k_buf)))]
    for copy in copies:
        copy.start()
    copies[0].wait()
    values = v_buf[...].astype(f32).T
    odd = lax.broadcasted_iota(jnp.int32, values.shape, 1) % 2
    mine_ref[...] = jnp.where(odd == core, values, 0.0).astype(bf16)
    others = jnp.where(odd == core, 0.0, values).astype(bf16)
    copies[1].wait()
    keys = k_buf[...]
    turns = []
    for j in range(4):
        turn = slab * 4 + j
        factor = jnp.where(turn == 0, 1.0, 2.0).astype(bf16)
        turns.append(keys * pltpu.roll(keys, lax.rem(DW - turn, DW), axis=1) * factor)
    turns.append(turned(keys, 64, 1))
    for j in range(0, 5, 2):
        feats = jnp.concatenate(turns[j : j + 2], axis=1)
        feats_ref[:, DW * j : DW * j + feats.shape[1]] = feats
        state = dot(others, feats).astype(bf16)
        for n in range(feats.shape[1] // DW):
            send_ref[j + n] = state[:, DW * n : DW * (n + 1)]


def mine_kernel(where_ref, feats_ref, values_ref, out_ref):
    for j in range(0, 5, 2):
        stop = min(5, j + 2)
        state = dot(values_ref[...], feats_ref[:, DW * j : DW * stop])
        for n in range(stop - j):
            out_ref[j + n] = state[:, DW * n : DW * (n + 1)]


def join_kernel(where_ref, mine_ref, got_ref, out_ref):
    for j in range(5):
        total = (mine_ref[j] + got_ref[j].astype(f32)).astype(bf16)
        if j < 4:
            out_ref[j, 0:DW, :] = total
        else:
            for n in range(4):
                out_ref[n, DW : DW + 32, :] = total[32 * n : 32 * n + 32]


def total_kernel(where_ref, in_ref, out_ref):
    total = in_ref[0].astype(f32)
    for n in range(1, in_ref.shape[0]):
        total = total + in_ref[n].astype(f32)
    out_ref[...] = total.astype(bf16)


EDGES = tuple((a, b) for a in range(4) for b in range(a + 1, 4))


def prefix_kernel(where_ref, in_ref, *refs):
    out_ref = refs[-1]
    total = jnp.zeros(out_ref.shape[1:], f32)
    for (_, to), ref in zip(EDGES, refs):
        total += jnp.where(where_ref[3] == to, ref[...].astype(f32), 0.0)
    for n in range(in_ref.shape[0]):
        out_ref[n] = total.astype(bf16)
        total = total + in_ref[n].astype(f32)


def part_kernel(where_ref, q_ref, k_ref, v_ref, mine_ref, send_ref, rows):
    core = where_ref[0]
    for n, ref in enumerate((q_ref, k_ref, v_ref)):
        rows[...] = ref[...].astype(f32)
        even = rows[pl.ds(0, 512, stride=2), :].astype(bf16)
        odd = rows[pl.ds(1, 512, stride=2), :].astype(bf16)
        mine_ref[n] = jnp.where(core == 0, even, odd)
        send_ref[n] = jnp.where(core == 0, odd, even)


def squared(q, k, v, causal):
    s = lax.dot_general(k, q, (((1,), (1,)), ((), ())), preferred_element_type=f32)
    s = s * s
    if causal:
        source = lax.broadcasted_iota(jnp.int32, s.shape, 0)
        token = lax.broadcasted_iota(jnp.int32, s.shape, 1)
        s = jnp.where(source <= token, s, 0.0)
    return dot(v.astype(f32).T.astype(bf16), s.astype(bf16))


def own_kernel(where_ref, mine_ref, theirs_ref, out0_ref, out1_ref, qkv, out):
    core = where_ref[0]
    qkv[0], qkv[1] = mine_ref[...], theirs_ref[...]
    for h in range(2):
        out[h] = squared(qkv[h, 0], qkv[h, 1], qkv[h, 2], True)
    late, early = 1 - core, core
    out[late] += squared(qkv[late, 0], qkv[early, 1], qkv[early, 2], False)
    out0_ref[...], out1_ref[...] = out[0], out[1]


def spread_kernel(where_ref, in_ref, pair_ref, own_ref, out_ref, last_ref):
    for n in range(4):
        piece = in_ref[n, 0:DW, :]
        for p in range(out_ref.shape[0]):
            out_ref[p, DW * n : DW * n + DW, :] = piece
        last_ref[32 * n : 32 * n + 32, :] = in_ref[n, DW : DW + 32, :]


def cross_kernel(where_ref, mine_ref, theirs_ref, pair_ref, state_ref, own0_ref, own1_ref, last_ref, out_ref):
    core, low = where_ref[0], where_ref[2]
    for block in range(2):
        for head in range(2):
            if head:
                q = pair_ref[block]
            else:
                q = (theirs_ref if block else mine_ref)[0]
            q = q.astype(f32).T.astype(bf16)
            ahead = jnp.where(low == 0, q, pltpu.roll(q, DW - 16, axis=0))
            if head:
                total = jnp.zeros((DW, q.shape[1]), f32)
            else:
                total = (own1_ref if block else own0_ref)[...] + dot(last_ref[...], turned(q, 64, 0))
            for p in range(8):
                turns = [32 * (p // 4) + 4 * (p % 4) + j for j in range(4)]
                feats = [q * (pltpu.roll(ahead, DW - t, axis=0) if t else ahead) for t in turns]
                state = [state_ref[p, DW * j : DW * (j + 1)] for j in range(4)]
                total += dot(jnp.concatenate(state, axis=1), jnp.concatenate(feats, axis=0))
            to_core = 1 - core if block else core
            to_low = 1 - low if head else low
            out_ref[2 * to_core + to_low] = total.astype(bf16)


def norm_kernel(where_ref, in_ref, out_ref, rows, buffer, sems):
    copies = []
    for n in range(2):
        at = slice(256 * n, 256 * n + 256)
        for kv in range(2):
            total = in_ref[2 * kv, :, at].astype(f32) + in_ref[2 * kv + 1, :, at].astype(f32)
            mean = jnp.mean(total * total, axis=0, keepdims=True)
            rows[pl.ds(512 * n + kv, 256, stride=2), :] = (total * lax.rsqrt(mean + 1e-06)).T
        at = slice(512 * n, 512 * n + 512)
        buffer[at, :] = rows[at, :].astype(bf16)
        copies.append(pltpu.make_async_copy(buffer.at[at], out_ref.at[at], sems.at[n]))
        copies[-1].start()
    for copy in copies:
        copy.wait()


def per_device(queries, keys, values):
    size = queries.shape[0]
    core = lax.axis_index("core")
    low = lax.axis_index("xl")
    slab = lax.axis_index("xh") * 8 + low * 4 + lax.axis_index("y")
    quarter = lax.axis_index("zh")
    where = jnp.stack([core, slab, low, quarter]).astype(jnp.int32)
    q, k, v = (a.reshape(2 * size, DW) for a in (queries, keys, values))
    buffer = pltpu.VMEM((2 * size, DW), bf16)
    send, feats, kept = call(
        send_kernel,
        [((5, DW, DW), bf16), ((2 * size, 5 * DW), bf16), ((DW, 2 * size), bf16)],
        where,
        [k, v],
        10**9,
        [buffer, buffer, pltpu.SemaphoreType.DMA((2,))],
        True,
    )
    got = lax.ppermute(send, "core", CORES)
    (mine,) = call(mine_kernel, [((5, DW, DW), f32)], where, [feats, kept], 10**9)
    chunks, chunk = ((4, 160, DW), bf16), ((160, DW), bf16)
    (state,) = call(join_kernel, [chunks], where, [mine, got], 10**6)

    def exchange(state):
        return lax.all_to_all(state, "zl", 0, 0)

    def turn(blocks, total):
        blocks = exchange(blocks)
        return blocks, call(total_kernel, [chunk], where, [blocks], 10**6)[0]

    blocks, total, passed = state, jnp.zeros(*chunk), []
    for n in range(4):
        blocks, total = lax.cond(quarter == n, turn, lambda *a: a, blocks, total)
        for a, b in EDGES:
            if a == n:
                passed.append(lax.ppermute(total, "zh", ((a, b),)))
    q, k, v, _ = lax.optimization_barrier((q, k, v, blocks))
    mine, send = call(
        part_kernel,
        [((3, size, DW), bf16), ((3, size, DW), bf16)],
        where,
        [q, k, v],
        10**8,
        [pltpu.VMEM((2 * size, DW), f32)],
    )
    theirs = lax.ppermute(send, "core", CORES)
    pair = lax.ppermute(jnp.stack([mine[0], theirs[0]]), "xl", CORES)
    own = call(
        own_kernel,
        [((DW, size), f32), ((DW, size), f32)],
        where,
        [mine, theirs],
        10**9,
        [pltpu.VMEM((2, 3, size, DW), bf16), pltpu.VMEM((2, DW, size), f32)],
    )
    (prefix,) = call(prefix_kernel, [chunks], where, [blocks, *passed], 10**6)
    entering = exchange(prefix)
    slabs, last = call(spread_kernel, [((8, 512, DW), bf16), ((DW, DW), bf16)], where, [entering, pair, own[0]], 10**6)
    gathered = lax.all_to_all(slabs, ("xh", "y"), 0, 0)
    (parts,) = call(cross_kernel, [((4, DW, size), bf16)], where, [mine, theirs, pair, gathered, *own, last], 4 * 10**9)
    parts = lax.all_to_all(parts, ("core", "xl"), 0, 0)
    (out,) = call(
        norm_kernel,
        [((2 * size, DW), bf16)],
        where,
        [parts],
        10**6,
        [pltpu.VMEM((2 * size, DW), f32), buffer, pltpu.SemaphoreType.DMA((2,))],
        raw_out=True,
    )
    return out.reshape(queries.shape)


def solution(mesh):
    grid = Mesh(mesh.devices.reshape(4, 4, 2, 2, 2, 4), ("zh", "zl", "core", "xh", "xl", "y"))
    seq, head = ("zh", "zl", "core"), ("xh", "xl", "y")
    return jax.shard_map(
        per_device,
        mesh=grid,
        in_specs=(P(seq, None, head, None), P(seq, None, None), P(seq, None, None)),
        out_specs=P(seq, None, head, None),
        check_vma=False,
    )
```

```python
import jax
import jax.numpy as jnp
from jax import lax
from jax.experimental import pallas as pl
from jax.experimental.pallas import tpu as pltpu
from jax.sharding import Mesh
from jax.sharding import PartitionSpec as P


DW = 128
CORES = ((0, 1), (1, 0))
SMEM = pltpu.MemorySpace.SMEM
VMEM = pltpu.MemorySpace.VMEM
HBM = pltpu.MemorySpace.HBM
bf16, f32 = jnp.bfloat16, jnp.float32


def call(body, outs, where, ins, flops=0, scratch=(), raw=0, raw_out=0):
    ispaces = [HBM if n < raw else VMEM for n in range(len(ins))]
    ospaces = [HBM if n < raw_out else VMEM for n in range(len(outs))]
    return pl.pallas_call(
        body,
        out_shape=[space(*out) for space, out in zip(ospaces, outs)],
        in_specs=[pl.BlockSpec(memory_space=space) for space in [SMEM, *ispaces]],
        out_specs=[pl.BlockSpec(memory_space=space) for space in ospaces],
        scratch_shapes=list(scratch),
        cost_estimate=pl.CostEstimate(flops=flops, transcendentals=0, bytes_accessed=1 << 20),
        compiler_params=pltpu.CompilerParams(vmem_limit_bytes=16 << 20),
    )(where, *[pltpu.with_memory_space_constraint(a, space) for a, space in zip(ins, ispaces)])


def dot(a, b):
    return jnp.dot(a, b, preferred_element_type=f32)


def turned(x, turn, axis):
    return x * pltpu.roll(x, (DW - turn) % DW, axis=axis) if turn % DW else x * x


def send_kernel(where_ref, k_ref, v_ref, send_ref, feats_ref, mine_ref, k_buf, v_buf, sems):
    core, slab = where_ref[0], where_ref[1]
    copies = [pltpu.make_async_copy(r, b, sems.at[n]) for n, (r, b) in enumerate(((v_ref, v_buf), (k_ref, k_buf)))]
    for copy in copies:
        copy.start()
    copies[0].wait()
    values = v_buf[...].astype(f32).T
    odd = lax.broadcasted_iota(jnp.int32, values.shape, 1) % 2
    mine_ref[...] = jnp.where(odd == core, values, 0.0).astype(bf16)
    others = jnp.where(odd == core, 0.0, values).astype(bf16)
    copies[1].wait()
    keys = k_buf[...]
    turns = []
    for j in range(4):
        turn = slab * 4 + j
        factor = jnp.where(turn == 0, 1.0, 2.0).astype(bf16)
        turns.append(keys * pltpu.roll(keys, lax.rem(DW - turn, DW), axis=1) * factor)
    turns.append(turned(keys, 64, 1))
    for j in range(0, 5, 2):
        feats = jnp.concatenate(turns[j : j + 2], axis=1)
        feats_ref[:, DW * j : DW * j + feats.shape[1]] = feats
        state = dot(others, feats).astype(bf16)
        for n in range(feats.shape[1] // DW):
            send_ref[j + n] = state[:, DW * n : DW * (n + 1)]


def mine_kernel(where_ref, feats_ref, values_ref, out_ref):
    for j in range(0, 5, 2):
        stop = min(5, j + 2)
        state = dot(values_ref[...], feats_ref[:, DW * j : DW * stop])
        for n in range(stop - j):
            out_ref[j + n] = state[:, DW * n : DW * (n + 1)]


def join_kernel(where_ref, mine_ref, got_ref, out_ref):
    for j in range(5):
        total = (mine_ref[j] + got_ref[j].astype(f32)).astype(bf16)
        if j < 4:
            out_ref[j, 0:DW, :] = total
        else:
            for n in range(4):
                out_ref[n, DW : DW + 32, :] = total[32 * n : 32 * n + 32]


def total_kernel(where_ref, in_ref, out_ref):
    total = in_ref[0].astype(f32)
    for n in range(1, in_ref.shape[0]):
        total = total + in_ref[n].astype(f32)
    out_ref[...] = total.astype(bf16)


EDGES = tuple((a, b) for a in range(4) for b in range(a + 1, 4))


def pass_kernel(where_ref, blocks_ref, total_ref):
    total_ref[0:16, :] = jnp.zeros((16, DW), bf16)


def prefix_kernel(where_ref, *refs):
    turns, edges, (out_ref, blocks, buffer, sems) = refs[:4], refs[4:-4], refs[-4:]
    count = blocks.shape[0]
    for quarter in range(4):

        @pl.when(where_ref[3] == quarter)
        def _():
            copy = pltpu.make_async_copy(turns[quarter], blocks, sems.at[count])
            copy.start()
            total = jnp.zeros(blocks.shape[1:], f32)
            for (_, to), ref in zip(EDGES, edges):
                if to == quarter:
                    total += ref[...].astype(f32)
            copy.wait()
            copies = []
            for n in range(count):
                buffer[n] = total.astype(bf16)
                copies.append(pltpu.make_async_copy(buffer.at[n], out_ref.at[n], sems.at[n]))
                copies[-1].start()
                total = total + blocks[n].astype(f32)
            for copy in copies:
                copy.wait()


def part_kernel(where_ref, q_ref, k_ref, v_ref, mine_ref, send_ref, rows):
    core = where_ref[0]
    for n, ref in enumerate((q_ref, k_ref, v_ref)):
        rows[...] = ref[...].astype(f32)
        even = rows[pl.ds(0, 512, stride=2), :].astype(bf16)
        odd = rows[pl.ds(1, 512, stride=2), :].astype(bf16)
        mine_ref[n] = jnp.where(core == 0, even, odd)
        send_ref[n] = jnp.where(core == 0, odd, even)


def squared(q, k, v, causal):
    s = lax.dot_general(k, q, (((1,), (1,)), ((), ())), preferred_element_type=f32)
    s = s * s
    if causal:
        source = lax.broadcasted_iota(jnp.int32, s.shape, 0)
        token = lax.broadcasted_iota(jnp.int32, s.shape, 1)
        s = jnp.where(source <= token, s, 0.0)
    return dot(v.astype(f32).T.astype(bf16), s.astype(bf16))


def own_kernel(where_ref, mine_ref, theirs_ref, out0_ref, out1_ref, qkv, out):
    core = where_ref[0]
    qkv[0], qkv[1] = mine_ref[...], theirs_ref[...]
    for h in range(2):
        out[h] = squared(qkv[h, 0], qkv[h, 1], qkv[h, 2], True)
    late, early = 1 - core, core
    out[late] += squared(qkv[late, 0], qkv[early, 1], qkv[early, 2], False)
    out0_ref[...], out1_ref[...] = out[0], out[1]


def spread_kernel(where_ref, in_ref, pair_ref, own_ref, out_ref, last_ref):
    for n in range(4):
        piece = in_ref[n, 0:DW, :]
        for p in range(out_ref.shape[0]):
            out_ref[p, DW * n : DW * n + DW, :] = piece
        last_ref[32 * n : 32 * n + 32, :] = in_ref[n, DW : DW + 32, :]


def cross_kernel(where_ref, mine_ref, theirs_ref, pair_ref, state_ref, own0_ref, own1_ref, last_ref, out_ref):
    core, low = where_ref[0], where_ref[2]
    for block in range(2):
        for head in range(2):
            if head:
                q = pair_ref[block]
            else:
                q = (theirs_ref if block else mine_ref)[0]
            q = q.astype(f32).T.astype(bf16)
            ahead = jnp.where(low == 0, q, pltpu.roll(q, DW - 16, axis=0))
            if head:
                total = jnp.zeros((DW, q.shape[1]), f32)
            else:
                total = (own1_ref if block else own0_ref)[...] + dot(last_ref[...], turned(q, 64, 0))
            for p in range(8):
                turns = [32 * (p // 4) + 4 * (p % 4) + j for j in range(4)]
                feats = [q * (pltpu.roll(ahead, DW - t, axis=0) if t else ahead) for t in turns]
                state = [state_ref[p, DW * j : DW * (j + 1)] for j in range(4)]
                total += dot(jnp.concatenate(state, axis=1), jnp.concatenate(feats, axis=0))
            to_core = 1 - core if block else core
            to_low = 1 - low if head else low
            out_ref[2 * to_core + to_low] = total.astype(bf16)


def norm_kernel(where_ref, in_ref, out_ref, rows, buffer, sems):
    copies = []
    for n in range(2):
        at = slice(256 * n, 256 * n + 256)
        for kv in range(2):
            total = in_ref[2 * kv, :, at].astype(f32) + in_ref[2 * kv + 1, :, at].astype(f32)
            mean = jnp.mean(total * total, axis=0, keepdims=True)
            rows[pl.ds(512 * n + kv, 256, stride=2), :] = (total * lax.rsqrt(mean + 1e-06)).T
        at = slice(512 * n, 512 * n + 512)
        buffer[at, :] = rows[at, :].astype(bf16)
        copies.append(pltpu.make_async_copy(buffer.at[at], out_ref.at[at], sems.at[n]))
        copies[-1].start()
    for copy in copies:
        copy.wait()


def per_device(queries, keys, values):
    size = queries.shape[0]
    core = lax.axis_index("core")
    low = lax.axis_index("xl")
    slab = lax.axis_index("xh") * 8 + low * 4 + lax.axis_index("y")
    quarter = lax.axis_index("zh")
    where = jnp.stack([core, slab, low, quarter]).astype(jnp.int32)
    q, k, v = (a.reshape(2 * size, DW) for a in (queries, keys, values))
    buffer = pltpu.VMEM((2 * size, DW), bf16)
    send, feats, kept = call(
        send_kernel,
        [((5, DW, DW), bf16), ((2 * size, 5 * DW), bf16), ((DW, 2 * size), bf16)],
        where,
        [k, v],
        10**9,
        [buffer, buffer, pltpu.SemaphoreType.DMA((2,))],
        raw=2,
    )
    got = lax.ppermute(send, "core", CORES)
    (mine,) = call(mine_kernel, [((5, DW, DW), f32)], where, [feats, kept], 10**9)
    chunks, chunk = ((4, 160, DW), bf16), ((160, DW), bf16)
    (state,) = call(join_kernel, [chunks], where, [mine, got], 10**6)

    def exchange(state):
        return lax.all_to_all(state, "zl", 0, 0)

    def turn(state):
        blocks = exchange(state)
        return blocks, call(total_kernel, [chunk], where, [blocks], 10**6)[0]

    def wait(state):
        return tuple(call(pass_kernel, [chunks, chunk], where, [], raw_out=1))

    turns, passed = [], []
    for n in range(4):
        blocks, total = lax.cond(quarter == n, turn, wait, state)
        turns.append(blocks)
        for a, b in EDGES:
            if a == n:
                passed.append(lax.ppermute(total, "zh", ((a, b),)))
    q, k, v, _ = lax.optimization_barrier((q, k, v, total))
    mine, send = call(
        part_kernel,
        [((3, size, DW), bf16), ((3, size, DW), bf16)],
        where,
        [q, k, v],
        10**8,
        [pltpu.VMEM((2 * size, DW), f32)],
    )
    theirs = lax.ppermute(send, "core", CORES)
    pair = lax.ppermute(jnp.stack([mine[0], theirs[0]]), "xl", CORES)
    own = call(
        own_kernel,
        [((DW, size), f32), ((DW, size), f32)],
        where,
        [mine, theirs],
        10**9,
        [pltpu.VMEM((2, 3, size, DW), bf16), pltpu.VMEM((2, DW, size), f32)],
    )
    (prefix,) = call(
        prefix_kernel,
        [chunks],
        where,
        [*turns, *passed],
        10**6,
        [pltpu.VMEM(*chunks), pltpu.VMEM(*chunks), pltpu.SemaphoreType.DMA((5,))],
        raw=4,
        raw_out=1,
    )
    entering = exchange(prefix)
    slabs, last = call(spread_kernel, [((8, 512, DW), bf16), ((DW, DW), bf16)], where, [entering, pair, own[0]], 10**6)
    gathered = lax.all_to_all(slabs, ("xh", "y"), 0, 0)
    (parts,) = call(cross_kernel, [((4, DW, size), bf16)], where, [mine, theirs, pair, gathered, *own, last], 4 * 10**9)
    parts = lax.all_to_all(parts, ("core", "xl"), 0, 0)
    (out,) = call(
        norm_kernel,
        [((2 * size, DW), bf16)],
        where,
        [parts],
        10**6,
        [pltpu.VMEM((2 * size, DW), f32), buffer, pltpu.SemaphoreType.DMA((2,))],
        raw_out=1,
    )
    return out.reshape(queries.shape)


def solution(mesh):
    grid = Mesh(mesh.devices.reshape(4, 4, 2, 2, 2, 4), ("zh", "zl", "core", "xh", "xl", "y"))
    seq, head = ("zh", "zl", "core"), ("xh", "xl", "y")
    return jax.shard_map(
        per_device,
        mesh=grid,
        in_specs=(P(seq, None, head, None), P(seq, None, None), P(seq, None, None)),
        out_specs=P(seq, None, head, None),
        check_vma=False,
    )
```

```python
import jax
import jax.numpy as jnp
from jax import lax
from jax.experimental import pallas as pl
from jax.experimental.pallas import tpu as pltpu
from jax.sharding import Mesh
from jax.sharding import PartitionSpec as P


DW = 128
CORES = ((0, 1), (1, 0))
SMEM = pltpu.MemorySpace.SMEM
VMEM = pltpu.MemorySpace.VMEM
HBM = pltpu.MemorySpace.HBM
bf16, f32 = jnp.bfloat16, jnp.float32


def call(body, outs, where, ins, flops=0, scratch=(), raw=0, raw_out=0):
    ispaces = [HBM if n < raw else VMEM for n in range(len(ins))]
    ospaces = [HBM if n < raw_out else VMEM for n in range(len(outs))]
    return pl.pallas_call(
        body,
        out_shape=[space(*out) for space, out in zip(ospaces, outs)],
        in_specs=[pl.BlockSpec(memory_space=space) for space in [SMEM, *ispaces]],
        out_specs=[pl.BlockSpec(memory_space=space) for space in ospaces],
        scratch_shapes=list(scratch),
        cost_estimate=pl.CostEstimate(flops=flops, transcendentals=0, bytes_accessed=1 << 20),
        compiler_params=pltpu.CompilerParams(vmem_limit_bytes=16 << 20),
    )(where, *[pltpu.with_memory_space_constraint(a, space) for a, space in zip(ins, ispaces)])


def dot(a, b):
    return jnp.dot(a, b, preferred_element_type=f32)


def turned(x, turn, axis):
    return x * pltpu.roll(x, (DW - turn) % DW, axis=axis) if turn % DW else x * x


def send_kernel(where_ref, k_ref, v_ref, send_ref, feats_ref, mine_ref, k_buf, v_buf, sems):
    core, slab = where_ref[0], where_ref[1]
    copies = [pltpu.make_async_copy(r, b, sems.at[n]) for n, (r, b) in enumerate(((v_ref, v_buf), (k_ref, k_buf)))]
    for copy in copies:
        copy.start()
    copies[0].wait()
    values = v_buf[...].astype(f32).T
    odd = lax.broadcasted_iota(jnp.int32, values.shape, 1) % 2
    mine_ref[...] = jnp.where(odd == core, values, 0.0).astype(bf16)
    others = jnp.where(odd == core, 0.0, values).astype(bf16)
    copies[1].wait()
    keys = k_buf[...]
    turns = []
    for j in range(4):
        turn = slab * 4 + j
        factor = jnp.where(turn == 0, 1.0, 2.0).astype(bf16)
        turns.append(keys * pltpu.roll(keys, lax.rem(DW - turn, DW), axis=1) * factor)
    turns.append(turned(keys, 64, 1))
    for j in range(0, 5, 2):
        feats = jnp.concatenate(turns[j : j + 2], axis=1)
        feats_ref[:, DW * j : DW * j + feats.shape[1]] = feats
        state = dot(others, feats).astype(bf16)
        for n in range(feats.shape[1] // DW):
            send_ref[j + n] = state[:, DW * n : DW * (n + 1)]


def mine_kernel(where_ref, feats_ref, values_ref, out_ref):
    for j in range(0, 5, 2):
        stop = min(5, j + 2)
        state = dot(values_ref[...], feats_ref[:, DW * j : DW * stop])
        for n in range(stop - j):
            out_ref[j + n] = state[:, DW * n : DW * (n + 1)]


def join_kernel(where_ref, mine_ref, got_ref, out_ref):
    for j in range(5):
        total = (mine_ref[j] + got_ref[j].astype(f32)).astype(bf16)
        if j < 4:
            out_ref[j, 0:DW, :] = total
        else:
            for n in range(4):
                out_ref[n, DW : DW + 32, :] = total[32 * n : 32 * n + 32]


def total_kernel(where_ref, in_ref, out_ref):
    total = in_ref[0].astype(f32)
    for n in range(1, in_ref.shape[0]):
        total = total + in_ref[n].astype(f32)
    out_ref[...] = total.astype(bf16)


EDGES = ((0, 1), (1, 2), (1, 3), (2, 3))


def add_kernel(where_ref, total_ref, before_ref, out_ref):
    before = jnp.where(where_ref[3] == 1, before_ref[...].astype(f32), 0.0)
    out_ref[...] = (total_ref[...].astype(f32) + before).astype(bf16)


def pass_kernel(where_ref, blocks_ref, total_ref):
    total_ref[0:16, :] = jnp.zeros((16, DW), bf16)


def prefix_kernel(where_ref, *refs):
    turns, edges, (out_ref, blocks, buffer, sems) = refs[:4], refs[4:-4], refs[-4:]
    count = blocks.shape[0]
    for quarter in range(4):

        @pl.when(where_ref[3] == quarter)
        def _():
            copies = []
            for n in range(count - 1):
                copies.append(pltpu.make_async_copy(turns[quarter].at[n], blocks.at[n], sems.at[count + n]))
                copies[-1].start()
            total = jnp.zeros(blocks.shape[1:], f32)
            for (_, to), ref in zip(EDGES, edges):
                if to == quarter:
                    total += ref[...].astype(f32)
            outs = []
            for n in range(count):
                buffer[n] = total.astype(bf16)
                outs.append(pltpu.make_async_copy(buffer.at[n], out_ref.at[n], sems.at[n]))
                outs[-1].start()
                if n < count - 1:
                    copies[n].wait()
                    total = total + blocks[n].astype(f32)
            for copy in outs:
                copy.wait()


def part_kernel(where_ref, q_ref, k_ref, v_ref, mine_ref, send_ref, rows):
    core = where_ref[0]
    for n, ref in enumerate((q_ref, k_ref, v_ref)):
        rows[...] = ref[...].astype(f32)
        even = rows[pl.ds(0, 512, stride=2), :].astype(bf16)
        odd = rows[pl.ds(1, 512, stride=2), :].astype(bf16)
        mine_ref[n] = jnp.where(core == 0, even, odd)
        send_ref[n] = jnp.where(core == 0, odd, even)


def squared(q, k, v, causal):
    s = lax.dot_general(k, q, (((1,), (1,)), ((), ())), preferred_element_type=f32)
    s = s * s
    if causal:
        source = lax.broadcasted_iota(jnp.int32, s.shape, 0)
        token = lax.broadcasted_iota(jnp.int32, s.shape, 1)
        s = jnp.where(source <= token, s, 0.0)
    return dot(v.astype(f32).T.astype(bf16), s.astype(bf16))


def own_kernel(where_ref, mine_ref, theirs_ref, out0_ref, out1_ref, qkv, out):
    core = where_ref[0]
    qkv[0], qkv[1] = mine_ref[...], theirs_ref[...]
    for h in range(2):
        out[h] = squared(qkv[h, 0], qkv[h, 1], qkv[h, 2], True)
    late, early = 1 - core, core
    out[late] += squared(qkv[late, 0], qkv[early, 1], qkv[early, 2], False)
    out0_ref[...], out1_ref[...] = out[0], out[1]


def spread_kernel(where_ref, in_ref, pair_ref, own_ref, out_ref, last_ref):
    for n in range(4):
        piece = in_ref[n, 0:DW, :]
        for p in range(out_ref.shape[0]):
            out_ref[p, DW * n : DW * n + DW, :] = piece
        last_ref[32 * n : 32 * n + 32, :] = in_ref[n, DW : DW + 32, :]


def cross_kernel(where_ref, mine_ref, theirs_ref, pair_ref, state_ref, own0_ref, own1_ref, last_ref, out_ref):
    core, low = where_ref[0], where_ref[2]
    for block in range(2):
        for head in range(2):
            if head:
                q = pair_ref[block]
            else:
                q = (theirs_ref if block else mine_ref)[0]
            q = q.astype(f32).T.astype(bf16)
            ahead = jnp.where(low == 0, q, pltpu.roll(q, DW - 16, axis=0))
            if head:
                total = jnp.zeros((DW, q.shape[1]), f32)
            else:
                total = (own1_ref if block else own0_ref)[...] + dot(last_ref[...], turned(q, 64, 0))
            for p in range(8):
                turns = [32 * (p // 4) + 4 * (p % 4) + j for j in range(4)]
                feats = [q * (pltpu.roll(ahead, DW - t, axis=0) if t else ahead) for t in turns]
                state = [state_ref[p, DW * j : DW * (j + 1)] for j in range(4)]
                total += dot(jnp.concatenate(state, axis=1), jnp.concatenate(feats, axis=0))
            to_core = 1 - core if block else core
            to_low = 1 - low if head else low
            out_ref[2 * to_core + to_low] = total.astype(bf16)


def norm_kernel(where_ref, in_ref, out_ref, rows, buffer, sems):
    copies = []
    for n in range(2):
        at = slice(256 * n, 256 * n + 256)
        for kv in range(2):
            total = in_ref[2 * kv, :, at].astype(f32) + in_ref[2 * kv + 1, :, at].astype(f32)
            mean = jnp.mean(total * total, axis=0, keepdims=True)
            rows[pl.ds(512 * n + kv, 256, stride=2), :] = (total * lax.rsqrt(mean + 1e-06)).T
        at = slice(512 * n, 512 * n + 512)
        buffer[at, :] = rows[at, :].astype(bf16)
        copies.append(pltpu.make_async_copy(buffer.at[at], out_ref.at[at], sems.at[n]))
        copies[-1].start()
    for copy in copies:
        copy.wait()


def per_device(queries, keys, values):
    size = queries.shape[0]
    core = lax.axis_index("core")
    low = lax.axis_index("xl")
    slab = lax.axis_index("xh") * 8 + low * 4 + lax.axis_index("y")
    quarter = lax.axis_index("zh")
    where = jnp.stack([core, slab, low, quarter]).astype(jnp.int32)
    q, k, v = (a.reshape(2 * size, DW) for a in (queries, keys, values))
    buffer = pltpu.VMEM((2 * size, DW), bf16)
    send, feats, kept = call(
        send_kernel,
        [((5, DW, DW), bf16), ((2 * size, 5 * DW), bf16), ((DW, 2 * size), bf16)],
        where,
        [k, v],
        10**9,
        [buffer, buffer, pltpu.SemaphoreType.DMA((2,))],
        raw=2,
    )
    got = lax.ppermute(send, "core", CORES)
    (mine,) = call(mine_kernel, [((5, DW, DW), f32)], where, [feats, kept], 10**9)
    chunks, chunk = ((4, 160, DW), bf16), ((160, DW), bf16)
    (state,) = call(join_kernel, [chunks], where, [mine, got], 10**6)

    def exchange(state):
        return lax.all_to_all(state, "zl", 0, 0)

    def turn(state):
        blocks = exchange(state)
        return blocks, call(total_kernel, [chunk], where, [blocks], 10**6)[0]

    def wait(state):
        return tuple(call(pass_kernel, [chunks, chunk], where, [], raw_out=1))

    turns, passed = [], []
    for n in range(4):
        blocks, total = lax.cond(quarter == n, turn, wait, state)
        turns.append(blocks)
        if n == 1:
            (total,) = call(add_kernel, [chunk], where, [total, passed[0]], 10**5)
        for a, b in EDGES:
            if a == n:
                passed.append(lax.ppermute(total, "zh", ((a, b),)))
    q, k, v, _ = lax.optimization_barrier((q, k, v, total))
    mine, send = call(
        part_kernel,
        [((3, size, DW), bf16), ((3, size, DW), bf16)],
        where,
        [q, k, v],
        10**8,
        [pltpu.VMEM((2 * size, DW), f32)],
    )
    theirs = lax.ppermute(send, "core", CORES)
    pair = lax.ppermute(jnp.stack([mine[0], theirs[0]]), "xl", CORES)
    own = call(
        own_kernel,
        [((DW, size), f32), ((DW, size), f32)],
        where,
        [mine, theirs],
        10**9,
        [pltpu.VMEM((2, 3, size, DW), bf16), pltpu.VMEM((2, DW, size), f32)],
    )
    (prefix,) = call(
        prefix_kernel,
        [chunks],
        where,
        [*turns, *passed],
        10**6,
        [pltpu.VMEM(*chunks), pltpu.VMEM(*chunks), pltpu.SemaphoreType.DMA((7,))],
        raw=4,
        raw_out=1,
    )
    entering = exchange(prefix)
    slabs, last = call(spread_kernel, [((8, 512, DW), bf16), ((DW, DW), bf16)], where, [entering, pair, own[0]], 10**6)
    gathered = lax.all_to_all(slabs, ("xh", "y"), 0, 0)
    (parts,) = call(cross_kernel, [((4, DW, size), bf16)], where, [mine, theirs, pair, gathered, *own, last], 4 * 10**9)
    parts = lax.all_to_all(parts, ("core", "xl"), 0, 0)
    (out,) = call(
        norm_kernel,
        [((2 * size, DW), bf16)],
        where,
        [parts],
        10**6,
        [pltpu.VMEM((2 * size, DW), f32), buffer, pltpu.SemaphoreType.DMA((2,))],
        raw_out=1,
    )
    return out.reshape(queries.shape)


def solution(mesh):
    grid = Mesh(mesh.devices.reshape(4, 4, 2, 2, 2, 4), ("zh", "zl", "core", "xh", "xl", "y"))
    seq, head = ("zh", "zl", "core"), ("xh", "xl", "y")
    return jax.shard_map(
        per_device,
        mesh=grid,
        in_specs=(P(seq, None, head, None), P(seq, None, None), P(seq, None, None)),
        out_specs=P(seq, None, head, None),
        check_vma=False,
    )
```

```python
import jax
import jax.numpy as jnp
from jax import lax
from jax.experimental import pallas as pl
from jax.experimental.pallas import tpu as pltpu
from jax.sharding import Mesh
from jax.sharding import PartitionSpec as P


DW = 128
CORES = ((0, 1), (1, 0))
SMEM = pltpu.MemorySpace.SMEM
VMEM = pltpu.MemorySpace.VMEM
HBM = pltpu.MemorySpace.HBM
bf16, f32 = jnp.bfloat16, jnp.float32


def call(body, outs, where, ins, flops=0, scratch=(), raw=0, raw_out=0):
    ispaces = [HBM if n < raw else VMEM for n in range(len(ins))]
    ospaces = [HBM if n < raw_out else VMEM for n in range(len(outs))]
    return pl.pallas_call(
        body,
        out_shape=[space(*out) for space, out in zip(ospaces, outs)],
        in_specs=[pl.BlockSpec(memory_space=space) for space in [SMEM, *ispaces]],
        out_specs=[pl.BlockSpec(memory_space=space) for space in ospaces],
        scratch_shapes=list(scratch),
        cost_estimate=pl.CostEstimate(flops=flops, transcendentals=0, bytes_accessed=1 << 20),
        compiler_params=pltpu.CompilerParams(vmem_limit_bytes=16 << 20),
    )(where, *[pltpu.with_memory_space_constraint(a, space) for a, space in zip(ins, ispaces)])


def dot(a, b):
    return jnp.dot(a, b, preferred_element_type=f32)


def turned(x, turn, axis):
    return x * pltpu.roll(x, (DW - turn) % DW, axis=axis) if turn % DW else x * x


def send_kernel(where_ref, k_ref, v_ref, send_ref, feats_ref, mine_ref, k_buf, v_buf, sems):
    core, slab = where_ref[0], where_ref[1]
    copies = [pltpu.make_async_copy(r, b, sems.at[n]) for n, (r, b) in enumerate(((v_ref, v_buf), (k_ref, k_buf)))]
    for copy in copies:
        copy.start()
    copies[0].wait()
    values = v_buf[...].astype(f32).T
    odd = lax.broadcasted_iota(jnp.int32, values.shape, 1) % 2
    mine_ref[...] = jnp.where(odd == core, values, 0.0).astype(bf16)
    others = jnp.where(odd == core, 0.0, values).astype(bf16)
    copies[1].wait()
    keys = k_buf[...]
    turns = []
    for j in range(4):
        turn = slab * 4 + j
        factor = jnp.where(turn == 0, 1.0, 2.0).astype(bf16)
        turns.append(keys * pltpu.roll(keys, lax.rem(DW - turn, DW), axis=1) * factor)
    turns.append(turned(keys, 64, 1))
    for j in range(0, 5, 2):
        feats = jnp.concatenate(turns[j : j + 2], axis=1)
        feats_ref[:, DW * j : DW * j + feats.shape[1]] = feats
        state = dot(others, feats).astype(bf16)
        for n in range(feats.shape[1] // DW):
            send_ref[j + n] = state[:, DW * n : DW * (n + 1)]


def mine_kernel(where_ref, feats_ref, values_ref, out_ref):
    for j in range(0, 5, 2):
        stop = min(5, j + 2)
        state = dot(values_ref[...], feats_ref[:, DW * j : DW * stop])
        for n in range(stop - j):
            out_ref[j + n] = state[:, DW * n : DW * (n + 1)]


def join_kernel(where_ref, mine_ref, got_ref, out_ref):
    for j in range(5):
        total = (mine_ref[j] + got_ref[j].astype(f32)).astype(bf16)
        if j < 4:
            out_ref[j, 0:DW, :] = total
        else:
            for n in range(4):
                out_ref[n, DW : DW + 32, :] = total[32 * n : 32 * n + 32]


def total_kernel(where_ref, in_ref, out_ref):
    total = in_ref[0].astype(f32)
    for n in range(1, in_ref.shape[0]):
        total = total + in_ref[n].astype(f32)
    out_ref[...] = total.astype(bf16)


EDGES = ((0, 1), (1, 2), (1, 3), (2, 3))


def add_kernel(where_ref, total_ref, before_ref, out_ref):
    before = jnp.where(where_ref[3] == 1, before_ref[...].astype(f32), 0.0)
    out_ref[...] = (total_ref[...].astype(f32) + before).astype(bf16)


def pass_kernel(where_ref, blocks_ref, total_ref):
    total_ref[0:16, :] = jnp.zeros((16, DW), bf16)


def prefix_kernel(where_ref, *refs):
    turns, edges, (out_ref, blocks, buffer, sems) = refs[:4], refs[4:-4], refs[-4:]
    count = blocks.shape[0]
    for quarter in range(4):

        @pl.when(where_ref[3] == quarter)
        def _():
            copies = []
            for n in range(count - 1):
                copies.append(pltpu.make_async_copy(turns[quarter].at[n], blocks.at[n], sems.at[count + n]))
                copies[-1].start()
            total = jnp.zeros(blocks.shape[1:], f32)
            for (_, to), ref in zip(EDGES, edges):
                if to == quarter:
                    total += ref[...].astype(f32)
            outs = []
            for n in range(count):
                buffer[n] = total.astype(bf16)
                outs.append(pltpu.make_async_copy(buffer.at[n], out_ref.at[n], sems.at[n]))
                outs[-1].start()
                if n < count - 1:
                    copies[n].wait()
                    total = total + blocks[n].astype(f32)
            for copy in outs:
                copy.wait()


def part_kernel(where_ref, q_ref, k_ref, v_ref, mine_ref, send_ref, rows):
    core = where_ref[0]
    for n, ref in enumerate((q_ref, k_ref, v_ref)):
        rows[...] = ref[...].astype(f32)
        even = rows[pl.ds(0, 512, stride=2), :].astype(bf16)
        odd = rows[pl.ds(1, 512, stride=2), :].astype(bf16)
        mine_ref[n] = jnp.where(core == 0, even, odd)
        send_ref[n] = jnp.where(core == 0, odd, even)


def squared(q, k, v, causal):
    s = lax.dot_general(k, q, (((1,), (1,)), ((), ())), preferred_element_type=f32)
    s = s * s
    if causal:
        source = lax.broadcasted_iota(jnp.int32, s.shape, 0)
        token = lax.broadcasted_iota(jnp.int32, s.shape, 1)
        s = jnp.where(source <= token, s, 0.0)
    return dot(v.astype(f32).T.astype(bf16), s.astype(bf16))


def own_kernel(where_ref, mine_ref, theirs_ref, out0_ref, out1_ref, qkv, out):
    core = where_ref[0]
    qkv[0], qkv[1] = mine_ref[...], theirs_ref[...]
    for h in range(2):
        out[h] = squared(qkv[h, 0], qkv[h, 1], qkv[h, 2], True)
    late, early = 1 - core, core
    out[late] += squared(qkv[late, 0], qkv[early, 1], qkv[early, 2], False)
    out0_ref[...], out1_ref[...] = out[0], out[1]


def spread_kernel(where_ref, in_ref, pair_ref, own_ref, out_ref, last_ref):
    for n in range(4):
        piece = in_ref[n, 0:DW, :]
        for p in range(out_ref.shape[0]):
            out_ref[p, DW * n : DW * n + DW, :] = piece
        last_ref[32 * n : 32 * n + 32, :] = in_ref[n, DW : DW + 32, :]


def cross_kernel(where_ref, mine_ref, theirs_ref, pair_ref, state_ref, own0_ref, own1_ref, last_ref, out_ref):
    core, low = where_ref[0], where_ref[2]
    for block in range(2):
        for head in range(2):
            if head:
                q = pair_ref[block]
            else:
                q = (theirs_ref if block else mine_ref)[0]
            q = q.astype(f32).T.astype(bf16)
            ahead = jnp.where(low == 0, q, pltpu.roll(q, DW - 16, axis=0))
            if head:
                total = jnp.zeros((DW, q.shape[1]), f32)
            else:
                total = (own1_ref if block else own0_ref)[...] + dot(last_ref[...], turned(q, 64, 0))
            for p in range(8):
                turns = [32 * (p // 4) + 4 * (p % 4) + j for j in range(4)]
                feats = [q * (pltpu.roll(ahead, DW - t, axis=0) if t else ahead) for t in turns]
                state = [state_ref[p, DW * j : DW * (j + 1)] for j in range(4)]
                total += dot(jnp.concatenate(state, axis=1), jnp.concatenate(feats, axis=0))
            to_core = 1 - core if block else core
            to_low = 1 - low if head else low
            out_ref[2 * to_core + to_low] = total.astype(bf16)


def norm_kernel(where_ref, in_ref, out_ref, rows, buffer, sems):
    copies = []
    for n in range(4):
        at = slice(DW * n, DW * n + DW)
        for kv in range(2):
            total = in_ref[2 * kv, :, at].astype(f32) + in_ref[2 * kv + 1, :, at].astype(f32)
            mean = jnp.mean(total * total, axis=0, keepdims=True)
            rows[pl.ds(256 * n + kv, DW, stride=2), :] = (total * lax.rsqrt(mean + 1e-06)).T
        at = slice(256 * n, 256 * n + 256)
        buffer[at, :] = rows[at, :].astype(bf16)
        copies.append(pltpu.make_async_copy(buffer.at[at], out_ref.at[at], sems.at[n]))
        copies[-1].start()
    for copy in copies:
        copy.wait()


def per_device(queries, keys, values):
    size = queries.shape[0]
    core = lax.axis_index("core")
    low = lax.axis_index("xl")
    slab = lax.axis_index("xh") * 8 + low * 4 + lax.axis_index("y")
    quarter = lax.axis_index("zh")
    where = jnp.stack([core, slab, low, quarter]).astype(jnp.int32)
    q, k, v = (a.reshape(2 * size, DW) for a in (queries, keys, values))
    buffer = pltpu.VMEM((2 * size, DW), bf16)
    send, feats, kept = call(
        send_kernel,
        [((5, DW, DW), bf16), ((2 * size, 5 * DW), bf16), ((DW, 2 * size), bf16)],
        where,
        [k, v],
        10**9,
        [buffer, buffer, pltpu.SemaphoreType.DMA((2,))],
        raw=2,
    )
    got = lax.ppermute(send, "core", CORES)
    (mine,) = call(mine_kernel, [((5, DW, DW), f32)], where, [feats, kept], 10**9)
    chunks, chunk = ((4, 160, DW), bf16), ((160, DW), bf16)
    (state,) = call(join_kernel, [chunks], where, [mine, got], 10**6)

    def exchange(state):
        return lax.all_to_all(state, "zl", 0, 0)

    def turn(state):
        blocks = exchange(state)
        return blocks, call(total_kernel, [chunk], where, [blocks], 10**6)[0]

    def wait(state):
        return tuple(call(pass_kernel, [chunks, chunk], where, [], raw_out=1))

    turns, passed = [], []
    for n in range(4):
        blocks, total = lax.cond(quarter == n, turn, wait, state)
        turns.append(blocks)
        if n == 1:
            (total,) = call(add_kernel, [chunk], where, [total, passed[0]], 10**5)
        for a, b in EDGES:
            if a == n:
                passed.append(lax.ppermute(total, "zh", ((a, b),)))
    q, k, v, _ = lax.optimization_barrier((q, k, v, total))
    mine, send = call(
        part_kernel,
        [((3, size, DW), bf16), ((3, size, DW), bf16)],
        where,
        [q, k, v],
        10**8,
        [pltpu.VMEM((2 * size, DW), f32)],
    )
    theirs = lax.ppermute(send, "core", CORES)
    pair = lax.ppermute(jnp.stack([mine[0], theirs[0]]), "xl", CORES)
    own = call(
        own_kernel,
        [((DW, size), f32), ((DW, size), f32)],
        where,
        [mine, theirs],
        10**9,
        [pltpu.VMEM((2, 3, size, DW), bf16), pltpu.VMEM((2, DW, size), f32)],
    )
    (prefix,) = call(
        prefix_kernel,
        [chunks],
        where,
        [*turns, *passed],
        10**6,
        [pltpu.VMEM(*chunks), pltpu.VMEM(*chunks), pltpu.SemaphoreType.DMA((7,))],
        raw=4,
        raw_out=1,
    )
    entering = exchange(prefix)
    slabs, last = call(spread_kernel, [((8, 512, DW), bf16), ((DW, DW), bf16)], where, [entering, pair, own[0]], 10**6)
    gathered = lax.all_to_all(slabs, ("xh", "y"), 0, 0)
    (parts,) = call(cross_kernel, [((4, DW, size), bf16)], where, [mine, theirs, pair, gathered, *own, last], 4 * 10**9)
    parts = lax.all_to_all(parts, ("core", "xl"), 0, 0)
    (out,) = call(
        norm_kernel,
        [((2 * size, DW), bf16)],
        where,
        [parts],
        10**6,
        [pltpu.VMEM((2 * size, DW), f32), buffer, pltpu.SemaphoreType.DMA((4,))],
        raw_out=1,
    )
    return out.reshape(queries.shape)


def solution(mesh):
    grid = Mesh(mesh.devices.reshape(4, 4, 2, 2, 2, 4), ("zh", "zl", "core", "xh", "xl", "y"))
    seq, head = ("zh", "zl", "core"), ("xh", "xl", "y")
    return jax.shard_map(
        per_device,
        mesh=grid,
        in_specs=(P(seq, None, head, None), P(seq, None, None), P(seq, None, None)),
        out_specs=P(seq, None, head, None),
        check_vma=False,
    )
```
